128 devices in a mesh: ctx: 32 (over x, y, core), vocab: 4 (over z).
Axes of the slice: x: 4, y: 4, z: 4, core: 2. Of those that a mesh axis runs over, the one named last changes fastest.
Arguments:
- query_rows: bfloat16 [8192, 4096], P('ctx', 'vocab'), may hold values from -12 to 12
- key_rows: bfloat16 [8192, 2048], P('ctx', 'vocab'), may hold values from -6 to 6
- value_rows: bfloat16 [8192, 2048], P('ctx', 'vocab'), may hold values from -6 to 6
- residual: bfloat16 [8192, 4608], P('ctx', 'vocab'), may hold values from -6 to 6
- out_weight: bfloat16 [4096, 4608], P('vocab'), may hold values from -0.09375 to 0.09375
- post_gain: float32 [4608], P('vocab'), may hold values from 0.1 to 1.9
- final_gain: float32 [4608], P('vocab'), may hold values from 0.1 to 1.9
- embedding: bfloat16 [131072, 4608], P(('ctx', 'vocab')), may hold values from -0.25 to 0.25
- targets: int32 [256], P('ctx'), may hold values from 0 to 131071
- loss_mask: int32 [256], P('ctx'), may hold values 0 or 1
- pick_pos: int32 [256], P('ctx'), may hold values from 0 to 255, as said below
Outputs:
- final_hidden: bfloat16 [8192, 4608], P('ctx', 'vocab')
- mean_loss: float32 [], replicated
- grad_normed: float32 [256, 4608], P('ctx', 'vocab')
The draws below stay inside these ranges and needn't reach their ends.
Inputs may be any that keep to these rules, and one draw needn't show every extreme that they name: `pick_pos`: entry k is a position inside the block of 256 tokens held by index k // 8 of ctx; entries may repeat.
All inputs are finite; a program needn't handle non-finite values. No bound on the sum of `loss_mask` on one device may be relied on, other than what follows from the above.
Results may differ from the reference program's by a relative error of at most 0.0049.
Values may be sent and summed in bfloat16 or wider, within the bound.
No kernel may reach another device: no remote copies, remote signals or barrier semaphores. Data moves between devices by JAX's collectives and lax.ppermute only.
A program may use at most 256 MiB of HBM per device.

```python
import math
import jax
import jax.numpy as jnp
import numpy as np
from jax import lax

D = 4608
HEADS = 32
KV_HEADS = 16
HEAD_DIM = 128
WINDOW = 4096
TOK_DEV = 256
PICK = 8
TOKENS = 8192
STRETCH = 256
VOCAB = 131072


def draw_pick_pos(key, part):
    values = jax.random.randint(key, (STRETCH,), 0, TOK_DEV, dtype=jnp.int32)
    values = values.at[0].set(0)
    return values.at[1].set(TOK_DEV - 1)


def place_ends(values, own_key, smallest, top_value):
    shape = values.shape
    index_at = [jax.random.randint(jax.random.fold_in(own_key, axis), (), 0, shape[axis]) for axis in range(len(shape))]
    values = values.at[tuple(index_at)].set(smallest)
    longest = shape.index(max(shape))
    index_at[longest] = (index_at[longest] + 1) % shape[longest]
    return values.at[tuple(index_at)].set(top_value)


def shard_levels(stream_key, shape, cuts, smallest, top_value):
    factor_of = 1.0
    for axis_at, parts in cuts:
        steps = jax.random.uniform(jax.random.fold_in(jax.random.fold_in(stream_key, 6), axis_at), (parts,), jnp.float32, smallest / len(cuts), top_value / len(cuts))
        factor_of = factor_of * jnp.repeat(jnp.exp(steps), shape[axis_at] // parts).reshape((-1,) + (1,) * (len(shape) - 1 - axis_at))
    return factor_of


def ranked_wide(own_key, extent, count, skew):
    portions = [min(1 << octave, count + 1 - (1 << octave)) * (1 << 20) // math.isqrt((1 << octave) ** skew) + 1 for octave in range((count + 1).bit_length()) if 1 << octave <= count]
    width = 1 + sum(portions) // (1 << 30)
    grid = np.cumsum(np.array([max(1, weight // width) for weight in portions]))
    pick = jax.random.randint(jax.random.fold_in(own_key, 1), extent, 0, int(grid[len(portions) - 1]))
    start = jnp.left_shift(1, jnp.searchsorted(jnp.asarray(grid, jnp.int32), pick, side="right").astype(jnp.int32))
    grade = start - 1 + jax.random.randint(jax.random.fold_in(own_key, 4), extent, 0, 1 << 30) % jnp.minimum(start, count + 1 - start)
    return jax.random.permutation(jax.random.fold_in(own_key, 2), count)[grade].astype(jnp.int32)


def normal_values(own_key, extent, spread, limit, split=(), held_as=jnp.bfloat16):
    entries = jax.random.normal(own_key, extent, jnp.float32) * spread
    if len(split) > 0:
        entries = shard_levels(own_key, extent, split, -0.22, 0.18) * entries
    return jnp.clip(entries, min=-limit, max=limit).astype(held_as)


def setup_inputs(seed: int = 0) -> dict:
    keys = jax.random.split(jax.random.key(seed), 12)
    query_rows = normal_values(keys[0], (TOKENS, HEADS * HEAD_DIM), 3.0, 12.0, ((0, 32), (1, 4)))
    key_rows = normal_values(keys[1], (TOKENS, KV_HEADS * HEAD_DIM), 1.0, 6.0, ((0, 32), (1, 4)))
    value_rows = normal_values(keys[2], (TOKENS, KV_HEADS * HEAD_DIM), 1.0, 6.0, ((0, 32), (1, 4)))
    residual = normal_values(keys[3], (TOKENS, D), 1.0, 6.0, ((0, 32), (1, 4)))
    out_weight = normal_values(keys[4], (HEADS * HEAD_DIM, D), (HEADS * HEAD_DIM) ** -0.5, 0.09375, ((0, 4),))
    post_gain = jnp.clip(1.0 + 0.18 * jax.random.normal(keys[5], (D,), jnp.float32), 0.1, 1.9)
    final_gain = jnp.clip(1.0 + 0.18 * jax.random.normal(keys[6], (D,), jnp.float32), 0.1, 1.9)
    embedding = normal_values(keys[7], (VOCAB, D), (D // 9) ** -0.5, 0.25, ((0, 128),))
    targets = place_ends(ranked_wide(keys[8], (STRETCH,), VOCAB, 2), jax.random.fold_in(keys[8], 3), 0, VOCAB - 1).astype(jnp.int32)
    loss_mask = place_ends((jax.random.randint(keys[9], (STRETCH,), 0, 8) < 7).astype(jnp.int32), jax.random.fold_in(keys[9], 1), 0, 1)
    pick_pos = draw_pick_pos(jax.random.fold_in(keys[11], 71), 0)
    return dict(query_rows=query_rows, key_rows=key_rows, value_rows=value_rows, residual=residual, out_weight=out_weight, post_gain=post_gain, final_gain=final_gain, embedding=embedding, targets=targets, loss_mask=loss_mask, pick_pos=pick_pos)


attn_cap = 50.0
logit_cap = 30.0
query_scalar = 144.0
epsilon = 1e-06

def attend_block(block_idx, query_rows, key_rows, value_rows):
    key_span = min(TOKENS, WINDOW + TOK_DEV)
    group_size = HEADS // KV_HEADS
    first_row = (block_idx * TOK_DEV).astype(jnp.int32)
    begin_row = jnp.clip(first_row + TOK_DEV - key_span, 0, TOKENS - key_span).astype(jnp.int32)
    query_blk = lax.dynamic_slice_in_dim(query_rows, first_row, TOK_DEV, 0).astype(jnp.float32)
    query_blk = query_blk.reshape(TOK_DEV, KV_HEADS, group_size, HEAD_DIM)
    key_blk = lax.dynamic_slice_in_dim(key_rows, begin_row, key_span, 0).astype(jnp.float32)
    key_blk = key_blk.reshape(key_span, KV_HEADS, HEAD_DIM)
    value_blk = lax.dynamic_slice_in_dim(value_rows, begin_row, key_span, 0).astype(jnp.float32)
    value_blk = value_blk.reshape(key_span, KV_HEADS, HEAD_DIM)
    raw_scores = jnp.einsum('tgcd,sgd->gcts', query_blk, key_blk)
    capped = attn_cap * jnp.tanh(raw_scores * query_scalar ** (-0.5) / attn_cap)
    query_pos = first_row + jnp.arange(TOK_DEV, dtype=jnp.int32)
    key_pos = begin_row + jnp.arange(key_span, dtype=jnp.int32)
    distance = query_pos[:, None] - key_pos[None, :]
    allowed = (distance >= 0) & (distance < WINDOW)
    weights = jnp.where(allowed, jnp.exp(capped), 0.0)
    denominator = lax.optimization_barrier(jnp.sum(weights, axis=-1))
    weights_low = lax.optimization_barrier(weights.astype(jnp.bfloat16)).astype(jnp.float32)
    numerator = jnp.einsum('gcts,sgd->gctd', weights_low, value_blk)
    attended = numerator / denominator[..., None]
    attended = jnp.transpose(attended, (2, 0, 1, 3)).reshape(TOK_DEV, HEADS * HEAD_DIM)
    return attended.astype(jnp.bfloat16)

def reference(query_rows, key_rows, value_rows, residual, out_weight, post_gain, final_gain, embedding, targets, loss_mask, pick_pos):

    def one_block(block_idx):
        return attend_block(block_idx, query_rows, key_rows, value_rows)
    attended = lax.map(one_block, jnp.arange(TOKENS // TOK_DEV, dtype=jnp.int32))
    attended = attended.reshape(TOKENS, HEADS * HEAD_DIM)
    projected = jnp.dot(attended, out_weight, preferred_element_type=jnp.float32)
    inv_rms = lax.rsqrt(lax.optimization_barrier(jnp.mean(projected * projected, axis=1, keepdims=True)) + epsilon)
    final_hidden = (residual.astype(jnp.float32) + projected * inv_rms * post_gain).astype(jnp.bfloat16)
    row_index = jnp.arange(STRETCH, dtype=jnp.int32) // PICK * TOK_DEV + pick_pos.astype(jnp.int32)
    picked = jnp.take(final_hidden, row_index, axis=0).astype(jnp.float32)
    picked_rms = lax.rsqrt(lax.optimization_barrier(jnp.mean(picked * picked, axis=1, keepdims=True)) + epsilon)
    normed = (picked * picked_rms * final_gain).astype(jnp.bfloat16)
    logits = jnp.dot(normed, embedding.T, preferred_element_type=jnp.float32)
    logits = logit_cap * jnp.tanh(logits / logit_cap)
    exp_logits = jnp.exp(logits)
    totals = lax.optimization_barrier(jnp.sum(exp_logits, axis=1))
    onehot = jnp.arange(VOCAB, dtype=jnp.int32)[None, :] == targets[:, None]
    target_logit = lax.optimization_barrier(jnp.sum(jnp.where(onehot, logits, 0.0), axis=1))
    mask_float = loss_mask.astype(jnp.float32)
    mean_loss = jnp.sum(mask_float * (jnp.log(totals) - target_logit)) / STRETCH
    dlogits = mask_float[:, None] * (exp_logits / totals[:, None] - onehot.astype(jnp.float32))
    dlogits = (dlogits * (1.0 - (logits / logit_cap) ** 2)).astype(jnp.bfloat16)
    grad_normed = jnp.dot(dlogits, embedding, preferred_element_type=jnp.float32)
    return (final_hidden, mean_loss, grad_normed)
```

```python
import functools

import jax
import jax.numpy as jnp
from jax import lax
from jax.experimental import pallas as pl
from jax.experimental.pallas import tpu as pltpu
from jax.sharding import Mesh
from jax.sharding import PartitionSpec as P

D = 4608
HEAD_DIM = 128
TOKENS = 8192
PICK = 8
SPAN = 512
BLK = 256
COLS = 1152
EXT = 128
LOSS_TOKENS = 256
CTX = ("x", "y", "core")

attn_cap = 50.0
logit_cap = 30.0
query_scalar = 144.0
epsilon = 1e-06

f32 = jnp.float32
bf16 = jnp.bfloat16


def ring(k):
    return [(j, (j + k) % 4) for j in range(4)]


SWAP = [(0, 1), (1, 0)]


def exchange(pieces, axes):
    return lax.all_to_all(pieces, axes, 0, 0, tiled=True)


def scores(q, k):
    return lax.dot_general(q, k, (((1,), (1,)), ((), ())), preferred_element_type=f32)


def weigh(raw):
    return jnp.exp(attn_cap * jnp.tanh(raw * (query_scalar**-0.5 / attn_cap)))


def lane_sums(p):
    parts = [p[:, i : i + 128] for i in range(0, p.shape[1], 128)]
    return functools.reduce(jnp.add, parts)


def load_kv(sc_ref, a_ref, b_ref, buf, sem):
    core = sc_ref[0]
    one = pltpu.make_async_copy(a_ref, buf.at[core], sem.at[0])
    two = pltpu.make_async_copy(b_ref, buf.at[1 - core], sem.at[1])
    one.start()
    two.start()
    one.wait()
    two.wait()


def add_full(q_ref, buf, acc_ref, first, rows, span):
    q = q_ref[0, rows, :]
    k = buf[0, pl.ds(first, span), :]
    v = buf[1, pl.ds(first, span), :]
    p = weigh(scores(q, k))
    acc_ref[0, rows, HEAD_DIM:] += lane_sums(p)
    acc_ref[0, rows, :HEAD_DIM] += jnp.dot(p.astype(bf16), v, preferred_element_type=f32)


def attn_own_kernel(sc_ref, q_ref, a_ref, b_ref, acc_ref, buf, sem):
    i = pl.program_id(0)

    @pl.when(i == 0)
    def _():
        load_kv(sc_ref, a_ref, b_ref, buf, sem)

    has_edge = i >= 2
    edge0 = jnp.maximum(i - 2, 0) * SPAN
    diag0 = i * SPAN
    tq = lax.broadcasted_iota(jnp.int32, (BLK, BLK), 0)
    tk = lax.broadcasted_iota(jnp.int32, (BLK, BLK), 1)
    causal = tk <= tq
    beyond = jnp.logical_and(jnp.logical_not(causal), has_edge)
    for r in range(2):
        rows = pl.ds(r * BLK, BLK)
        q = q_ref[0, rows, :]
        kd = buf[0, pl.ds(diag0 + r * BLK, BLK), :]
        ke = buf[0, pl.ds(edge0 + r * BLK, BLK), :]
        vd = buf[1, pl.ds(diag0 + r * BLK, BLK), :]
        ve = buf[1, pl.ds(edge0 + r * BLK, BLK), :]
        p = weigh(jnp.where(causal, scores(q, kd), scores(q, ke)))
        pd = jnp.where(causal, p, 0.0)
        pe = jnp.where(beyond, p, 0.0)
        acc_ref[0, rows, HEAD_DIM:] = lane_sums(pd) + lane_sums(pe)
        acc_ref[0, rows, :HEAD_DIM] = jnp.dot(
            pd.astype(bf16), vd, preferred_element_type=f32
        ) + jnp.dot(pe.astype(bf16), ve, preferred_element_type=f32)
    add_full(q_ref, buf, acc_ref, diag0, pl.ds(BLK, BLK), BLK)

    @pl.when(has_edge)
    def _():
        add_full(q_ref, buf, acc_ref, edge0 + BLK, pl.ds(0, BLK), BLK)

    @pl.when(i >= 1)
    def _():
        for r in range(2):
            add_full(q_ref, buf, acc_ref, (i - 1) * SPAN, pl.ds(r * BLK, BLK), SPAN)


def attn_more_kernel(last, sc_ref, q_ref, a_ref, b_ref, in_ref, out_ref, buf, sem, *scr):
    i = pl.program_id(0)
    acc_ref = scr[0] if last else out_ref

    @pl.when(i == 0)
    def _():
        load_kv(sc_ref, a_ref, b_ref, buf, sem)

    acc_ref[...] = in_ref[...]
    for step in range(2):
        at = i - sc_ref[1] - step

        @pl.when(at >= 0)
        def _():
            for r in range(2):
                add_full(q_ref, buf, acc_ref, at * SPAN, pl.ds(r * BLK, BLK), SPAN)

    if last:
        whole = jnp.sum(acc_ref[0, :, HEAD_DIM:], axis=1, keepdims=True)
        done = (acc_ref[0, :, :HEAD_DIM] / whole).astype(bf16)
        for z in range(4):
            out_ref[z, 0] = done


def attn_call(scalars, q, a, b, acc=None, last=False):
    q_spec = pl.BlockSpec((1, SPAN, HEAD_DIM), lambda i, sc: (i, 0, 0))
    acc_spec = pl.BlockSpec((1, SPAN, 2 * HEAD_DIM), lambda i, sc: (i, 0, 0))
    hbm = pl.BlockSpec(memory_space=pl.ANY)
    scratch = [pltpu.VMEM((2, 4 * SPAN, HEAD_DIM), bf16), pltpu.SemaphoreType.DMA((2,))]
    out_spec, out_shape = acc_spec, jax.ShapeDtypeStruct((4, SPAN, 2 * HEAD_DIM), f32)
    in_specs, args = [q_spec, hbm, hbm], [q, a, b]
    kernel = attn_own_kernel
    if acc is not None:
        in_specs, args = in_specs + [acc_spec], args + [acc]
        kernel = functools.partial(attn_more_kernel, last)
    if last:
        out_spec = pl.BlockSpec((4, 1, SPAN, HEAD_DIM), lambda i, sc: (0, i, 0, 0))
        out_shape = jax.ShapeDtypeStruct((4, 4, SPAN, HEAD_DIM), bf16)
        scratch = scratch + [pltpu.VMEM((1, SPAN, 2 * HEAD_DIM), f32)]
    return pl.pallas_call(
        kernel,
        out_shape=out_shape,
        grid_spec=pltpu.PrefetchScalarGridSpec(
            num_scalar_prefetch=1,
            grid=(4,),
            in_specs=in_specs,
            out_specs=out_spec,
            scratch_shapes=scratch,
        ),
        compiler_params=pltpu.CompilerParams(dimension_semantics=("arbitrary",)),
    )(scalars, *args)


def proj_kernel(
    sc_ref, pick_ref, att_ref, w_ref, a1, a2, a3, b1, b2, b3, rp_ref, pg_ref, fg_ref,
    own_ref, zp_ref, abuf, wbuf, asem, wsem,
):
    zi, ci = sc_ref[0], sc_ref[1]
    heads = [zi * 2, zi * 2 + 1]
    heads += [((zi - s + 4) % 4) * 2 + ci for s in (1, 2, 3)]
    heads += [((zi - s + 4) % 4) * 2 + 1 - ci for s in (1, 2, 3)]
    col = pl.multiple_of(zi * COLS, 128)
    src = [w_ref.at[pl.ds(0, 512), pl.ds(col, COLS)], w_ref.at[pl.ds(512, 512), pl.ds(col, COLS)]]
    src += [a1, a2, a3, b1, b2, b3]
    acopies, wcopies = [], []
    for n in range(8):
        acopies.append(
            pltpu.make_async_copy(att_ref.at[pl.ds(heads[n] * 4, 4)], abuf.at[n], asem.at[n])
        )
        wcopies.append(pltpu.make_async_copy(src[n], wbuf.at[n], wsem.at[n]))
        acopies[n].start()
        wcopies[n].start()
    for n in range(8):
        acopies[n].wait()
        wcopies[n].wait()
        lhs = jnp.concatenate([abuf[n, h] for h in range(4)], axis=1)
        part = jnp.dot(lhs, wbuf[n], preferred_element_type=f32)
        if n == 0:
            own_ref[...] = part
        else:
            own_ref[...] += part
    own = own_ref[...]
    squares = lax.dot_general(
        jnp.ones((8, COLS), f32), own * own, (((1,), (1,)), ((), ())),
        preferred_element_type=f32, precision=lax.Precision.HIGHEST,
    )
    for z in range(4):
        for p in range(PICK):
            zp_ref[z, p : p + 1, :] = own_ref[pl.ds(pick_ref[p], 1), :]
        zp_ref[z, 8:16, :] = rp_ref[...]
        zp_ref[z, 16:17, :] = pg_ref[...]
        zp_ref[z, 17:18, :] = fg_ref[...]
        zp_ref[z, 18:24, :] = jnp.zeros((6, COLS), f32)
        zp_ref[z, 18:19, :LOSS_TOKENS] = squares[:1]


def project(scalars, pick, att, w, parts, res_pick, pg, fg):
    hbm = pl.BlockSpec(memory_space=pl.ANY)
    whole = lambda *dims: pl.BlockSpec(dims, lambda i, *sc: (0,) * len(dims))
    return pl.pallas_call(
        proj_kernel,
        out_shape=(
            jax.ShapeDtypeStruct((BLK, COLS), f32),
            jax.ShapeDtypeStruct((4, 24, COLS), f32),
        ),
        grid_spec=pltpu.PrefetchScalarGridSpec(
            num_scalar_prefetch=2,
            grid=(1,),
            in_specs=[hbm] * 8 + [whole(PICK, COLS), whole(1, COLS), whole(1, COLS)],
            out_specs=(whole(BLK, COLS), whole(4, 24, COLS)),
            scratch_shapes=[
                pltpu.VMEM((8, 4, BLK, HEAD_DIM), bf16),
                pltpu.VMEM((8, 512, COLS), bf16),
                pltpu.SemaphoreType.DMA((8,)),
                pltpu.SemaphoreType.DMA((8,)),
            ],
        ),
        compiler_params=pltpu.CompilerParams(dimension_semantics=("arbitrary",)),
    )(scalars, pick, att, w, *parts, res_pick, pg, fg)


def norm_kernel(zr_ref, ext_ref, out_ref):
    own = [zr_ref[z, :8, :] for z in range(4)]
    total = sum(jnp.sum(o * o, axis=1, keepdims=True) for o in own)
    inv = lax.rsqrt(total / D + epsilon)
    picked = [
        (zr_ref[z, 8:16, :] + own[z] * inv * zr_ref[z, 16:17, :]).astype(bf16).astype(f32)
        for z in range(4)
    ]
    total = sum(jnp.sum(o * o, axis=1, keepdims=True) for o in picked)
    inv = lax.rsqrt(total / D + epsilon)
    for z in range(4):
        normed = (picked[z] * inv * zr_ref[z, 17:18, :]).astype(bf16)
        for n in range(16):
            out_ref[n, :, z * COLS : (z + 1) * COLS] = normed
    for n in range(16):
        out_ref[n, :, D:] = ext_ref[...]


def normalise(zr, ext):
    return pl.pallas_call(
        norm_kernel, out_shape=jax.ShapeDtypeStruct((16, PICK, D + EXT), bf16)
    )(zr, ext)


def loss_kernel(sc_ref, g_ref, s_ref, e_ref, out_ref, row_ref, nbuf, acc):
    j = pl.program_id(0)

    @pl.when(j == 0)
    def _():
        nbuf[:128] = g_ref[...]
        nbuf[128:] = s_ref[...]

    emb = e_ref[...]
    raw = scores(nbuf[:, :D], emb)
    bent = jnp.tanh(raw / logit_cap)
    logits = logit_cap * bent
    big = jnp.exp(logits)
    code = nbuf[:, D:].astype(f32)
    target = code[:, 0:1] * 16384.0 + code[:, 1:2] * 128.0 + code[:, 2:3]
    at = lax.broadcasted_iota(jnp.int32, (LOSS_TOKENS, BLK), 1) + (sc_ref[0] + j * BLK)
    hit = at == target.astype(jnp.int32)
    left = jnp.concatenate(
        [(big * (1.0 - bent * bent)).astype(bf16), jnp.where(hit, 1.0, 0.0).astype(bf16)], axis=0
    )
    ones = jnp.ones((8, BLK), f32)
    row_sum = lambda m: lax.dot_general(
        ones, m, (((1,), (1,)), ((), ())),
        preferred_element_type=f32, precision=lax.Precision.HIGHEST,
    )
    totals = row_sum(big)
    hits = row_sum(jnp.where(hit, logits, 0.0))
    both = jnp.concatenate([totals[:1], hits[:1], jnp.zeros((6, LOSS_TOKENS), f32)], axis=0)

    @pl.when(j == 0)
    def _():
        acc[...] = jnp.dot(left, emb, preferred_element_type=f32)
        row_ref[...] = both

    @pl.when(j > 0)
    def _():
        acc[...] += jnp.dot(left, emb, preferred_element_type=f32)
        row_ref[...] += both

    @pl.when(j == 3)
    def _():
        for h in range(2):
            for z in range(4):
                for part in range(2):
                    out_ref[h, z, :, part * COLS : (part + 1) * COLS] = acc[
                        part * 256 + h * 128 : part * 256 + h * 128 + 128, z * COLS : (z + 1) * COLS
                    ].astype(bf16)


def loss_parts(scalars, g, s, emb):
    whole = lambda *dims: pl.BlockSpec(dims, lambda i, sc: (0,) * len(dims))
    return pl.pallas_call(
        loss_kernel,
        out_shape=(
            jax.ShapeDtypeStruct((2, 4, 128, 2 * COLS), bf16),
            jax.ShapeDtypeStruct((8, LOSS_TOKENS), f32),
        ),
        grid_spec=pltpu.PrefetchScalarGridSpec(
            num_scalar_prefetch=1,
            grid=(4,),
            in_specs=[
                whole(128, D + EXT),
                whole(128, D + EXT),
                pl.BlockSpec((BLK, D), lambda i, sc: (i, 0)),
            ],
            out_specs=(whole(2, 4, 128, 2 * COLS), whole(8, LOSS_TOKENS)),
            scratch_shapes=[
                pltpu.VMEM((LOSS_TOKENS, D + EXT), bf16),
                pltpu.VMEM((2 * LOSS_TOKENS, D), f32),
            ],
        ),
        compiler_params=pltpu.CompilerParams(dimension_semantics=("arbitrary",)),
    )(scalars, g, s, emb)


def shards(
    query_rows, key_rows, value_rows, residual, out_weight, post_gain, final_gain,
    embedding, targets, loss_mask, pick_pos,
):
    xi, yi, ci, zi = (lax.axis_index(a) for a in ("x", "y", "core", "vocab"))
    i32 = lambda *v: jnp.stack([jnp.asarray(e, jnp.int32) for e in v])

    q_heads = query_rows.reshape(BLK, 8, HEAD_DIM).transpose(1, 0, 2)
    k_heads = key_rows.reshape(BLK, 4, HEAD_DIM).transpose(1, 0, 2)
    v_heads = value_rows.reshape(BLK, 4, HEAD_DIM).transpose(1, 0, 2)
    kv = jnp.stack([k_heads, v_heads], axis=1).reshape(8, BLK, HEAD_DIM)
    got = exchange(jnp.concatenate([q_heads, kv], axis=1), ("x", "core"))
    q = got[:, :BLK].reshape(4, SPAN, HEAD_DIM)
    own = got[:, BLK:].reshape(4 * SPAN, HEAD_DIM)

    swap = lambda a: lax.ppermute(a, "core", SWAP)
    down, up, far = (lax.ppermute(own, "y", ring(k)) for k in (1, 3, 2))

    sent = [
        lax.dynamic_slice(out_weight, (ci * 512, ((zi + s) % 4) * COLS), (512, COLS))
        for s in (1, 2, 3)
    ]
    mine = [lax.ppermute(p, "vocab", ring(s)) for p, s in zip(sent, (1, 2, 3))]
    theirs = [swap(p) for p in mine]

    acc = attn_call(i32(ci, 0), q, own, swap(own))
    acc = attn_call(i32(ci, jnp.where(yi >= 1, 0, 1)), q, down, swap(down), acc)
    acc = attn_call(i32(ci, jnp.where(yi == 3, 0, 1)), q, up, swap(up), acc)
    out = attn_call(i32(ci, jnp.where(yi >= 2, 0, 1)), q, far, swap(far), acc, last=True)
    att = exchange(out.reshape(32, BLK, HEAD_DIM), ("vocab", "x", "core"))

    res_pick = jnp.take(residual, pick_pos, axis=0).astype(f32)
    own_cols, zp = project(
        i32(zi, ci), pick_pos, att, out_weight, mine + theirs,
        res_pick, post_gain[None], final_gain[None],
    )
    zr = exchange(zp, "vocab")
    square_sum = jnp.sum(zr[:, 18, :LOSS_TOKENS], axis=0)
    inv_rms = lax.rsqrt(square_sum / D + epsilon)[:, None]
    final_hidden = (residual.astype(f32) + own_cols * inv_rms * post_gain).astype(bf16)

    coded = jnp.stack([targets >> 14, (targets >> 7) & 127, targets & 127, loss_mask], axis=1)
    ext = jnp.pad(coded, ((0, 0), (0, EXT - 4))).astype(bf16)
    g = exchange(normalise(zr, ext), ("x", "y")).reshape(128, D + EXT)
    vocab_local = embedding.shape[0]
    base = (((xi * 4 + yi) * 2 + ci) * 4 + zi) * vocab_local
    parts, rows = loss_parts(i32(base), g, swap(g), embedding)

    summed = (parts[0].astype(f32) + swap(parts[1]).astype(f32)).astype(bf16)
    row = rows[:2, :128] + swap(rows[:2, 128:])
    high = lax.reduce_precision(row, 8, 7)
    low = row - high
    info = jnp.stack([high[0], low[0], high[1], low[1]] + [jnp.zeros((128,), f32)] * 4)
    info = jnp.broadcast_to(info.astype(bf16)[None], (64, 8, 128))
    back = exchange(
        jnp.concatenate([summed.reshape(64, 8, 2 * COLS), info], axis=2), ("vocab", "x", "y")
    ).astype(f32)
    facts = jnp.sum(back[:, :4, 2 * COLS :], axis=0)
    totals, target_logit = facts[0] + facts[1], facts[2] + facts[3]
    masks = g[:, D + 3].astype(f32)
    loss = jnp.sum(masks * (jnp.log(totals) - target_logit)) / LOSS_TOKENS
    loss = loss + lax.ppermute(loss[None], "core", SWAP)[0]

    sums = jnp.sum(back[:, :, : 2 * COLS], axis=0)
    at = (xi * 4 + yi) * PICK
    my_total = lax.dynamic_slice(totals, (at,), (PICK,))[:, None]
    my_logit = lax.dynamic_slice(target_logit, (at,), (PICK,))[:, None]
    slope = 1.0 - (my_logit / logit_cap) ** 2
    grad = loss_mask.astype(f32)[:, None] * (sums[:, :COLS] / my_total - slope * sums[:, COLS:])
    return (final_hidden, loss, grad)


def solution(mesh):
    split = Mesh(
        mesh.devices.reshape(4, 4, 2, mesh.shape["vocab"]), ("x", "y", "core", "vocab")
    )
    return jax.shard_map(
        shards,
        mesh=split,
        in_specs=(
            P(CTX, "vocab"),
            P(CTX, "vocab"),
            P(CTX, "vocab"),
            P(CTX, "vocab"),
            P("vocab", None),
            P("vocab"),
            P("vocab"),
            P((*CTX, "vocab"), None),
            P(CTX),
            P(CTX),
            P(CTX),
        ),
        out_specs=(P(CTX, "vocab"), P(), P(CTX, "vocab")),
        check_vma=False,
    )
```

```python
import functools

import jax
import jax.numpy as jnp
from jax import lax
from jax.experimental import pallas as pl
from jax.experimental.pallas import tpu as pltpu
from jax.sharding import Mesh
from jax.sharding import PartitionSpec as P


D = 4608
HEAD_DIM = 128
PICK = 8
SPAN = 512
BLK = 256
COLS = 1152
EXT = 128
LOSS_TOKENS = 256
CTX = ("x", "y", "core")

attn_cap = 50.0
logit_cap = 30.0
query_scalar = 144.0
epsilon = 1e-06

f32 = jnp.float32
bf16 = jnp.bfloat16


def ring(k):
    return [(j, (j + k) % 4) for j in range(4)]


SWAP = [(0, 1), (1, 0)]


def exchange(pieces, axes):
    return lax.all_to_all(pieces, axes, 0, 0, tiled=True)


def scores(q, k):
    return lax.dot_general(q, k, (((1,), (1,)), ((), ())), preferred_element_type=f32)


def weigh(raw):
    return jnp.exp(attn_cap * jnp.tanh(raw * (query_scalar**-0.5 / attn_cap)))


def lane_sums(p):
    parts = [p[:, i : i + 128] for i in range(0, p.shape[1], 128)]
    return functools.reduce(jnp.add, parts)


def load_kv(core, a_ref, b_ref, buf, sem):
    copies = [
        pltpu.make_async_copy(a_ref, buf.at[core], sem.at[0]),
        pltpu.make_async_copy(b_ref, buf.at[1 - core], sem.at[1]),
    ]
    for copy in copies:
        copy.start()
    return copies


def seen(q, buf, first, span, valid=None):
    p = weigh(scores(q, buf[0, pl.ds(first, span), :]))
    if valid is not None:
        half = span // 2
        p = jnp.concatenate([p[:, :half], jnp.where(valid, p[:, half:], 0.0)], axis=1)
    v = buf[1, pl.ds(first, span), :]
    return jnp.dot(p.astype(bf16), v, preferred_element_type=f32), lane_sums(p)


def attn_own_kernel(sc_ref, q_ref, a_ref, b_ref, acc_ref, buf, sem):
    i = pl.program_id(0)

    @pl.when(i == 0)
    def _():
        for copy in load_kv(sc_ref[1], a_ref, b_ref, buf, sem):
            copy.wait()

    def body(earlier):
        has_edge = i >= 2
        edge0 = jnp.maximum(i - 2, 0) * SPAN
        diag0 = i * SPAN
        tq = lax.broadcasted_iota(jnp.int32, (BLK, BLK), 0)
        tk = lax.broadcasted_iota(jnp.int32, (BLK, BLK), 1)
        causal = tk <= tq
        beyond = jnp.logical_and(jnp.logical_not(causal), has_edge)
        for r in range(2):
            q = q_ref[0, pl.ds(r * BLK, BLK), :]
            raw = scores(q, buf[0, pl.ds(diag0 + r * BLK, BLK), :])
            if earlier:
                raw = jnp.where(causal, raw, scores(q, buf[0, pl.ds(edge0 + r * BLK, BLK), :]))
            p = weigh(raw)
            pd = jnp.where(causal, p, 0.0)
            top = jnp.dot(
                pd.astype(bf16), buf[1, pl.ds(diag0 + r * BLK, BLK), :], preferred_element_type=f32
            )
            low = lane_sums(pd)
            if earlier:
                pe = jnp.where(beyond, p, 0.0)
                top += jnp.dot(
                    pe.astype(bf16), buf[1, pl.ds(edge0 + r * BLK, BLK), :],
                    preferred_element_type=f32,
                )
                low += lane_sums(pe)
                more = seen(q, buf, (i - 1) * SPAN, SPAN)
                top, low = top + more[0], low + more[1]
            if r == 1:
                more = seen(q, buf, diag0, BLK)
                top, low = top + more[0], low + more[1]
            elif earlier:
                p = jnp.where(has_edge, weigh(scores(q, buf[0, pl.ds(edge0 + BLK, BLK), :])), 0.0)
                top += jnp.dot(
                    p.astype(bf16), buf[1, pl.ds(edge0 + BLK, BLK), :], preferred_element_type=f32
                )
                low += lane_sums(p)
            acc_ref[0, pl.ds(r * BLK, BLK), :HEAD_DIM] = top
            acc_ref[0, pl.ds(r * BLK, BLK), HEAD_DIM:] = low

    pl.when(i == 0)(lambda: body(False))
    pl.when(i > 0)(lambda: body(True))


def attn_more_kernel(chunks, last, at, sc_ref, q_ref, *refs):
    keys, (in_ref, out_ref, buf, sem, *scr) = refs[: 2 * chunks], refs[2 * chunks :]
    i = pl.program_id(0)
    acc_ref = scr[0] if last else out_ref

    @pl.when(i == 0)
    def _():
        copies = []
        for n in range(chunks):
            copies += load_kv(sc_ref[1], keys[2 * n], keys[2 * n + 1], buf.at[n], sem.at[n])
        for copy in copies:
            copy.wait()
        acc_ref[...] = in_ref[...]

    for n in range(chunks):

        @pl.when(jnp.logical_and(i == 0, sc_ref[at + n] == 0))
        def _():
            for r in range(2):
                rows = pl.ds(r * BLK, BLK)
                top, low = seen(q_ref[0, rows, :], buf.at[n], 0, SPAN)
                acc_ref[0, rows, :HEAD_DIM] += top
                acc_ref[0, rows, HEAD_DIM:] += low

    @pl.when(i > 0)
    def _():
        for r in range(2):
            rows = pl.ds(r * BLK, BLK)
            q = q_ref[0, rows, :]
            top, low = in_ref[0, rows, :HEAD_DIM], in_ref[0, rows, HEAD_DIM:]
            for n in range(chunks):
                newest = i - sc_ref[at + n]
                first = jnp.maximum(newest - 1, 0) * SPAN
                more = seen(q, buf.at[n], first, 2 * SPAN, newest > 0)
                top, low = top + more[0], low + more[1]
            acc_ref[0, rows, :HEAD_DIM] = top
            acc_ref[0, rows, HEAD_DIM:] = low

    if last:
        whole = jnp.sum(acc_ref[0, :, HEAD_DIM:], axis=1, keepdims=True)
        done = (acc_ref[0, :, :HEAD_DIM] / whole).astype(bf16)
        for z in range(4):
            out_ref[z, 0] = done


def attn_call(scalars, q, keys, acc=None, at=0, last=False):
    q_spec = pl.BlockSpec((1, SPAN, HEAD_DIM), lambda i, sc: (i, 0, 0))
    acc_spec = pl.BlockSpec((1, SPAN, 2 * HEAD_DIM), lambda i, sc: (i, 0, 0))
    hbm = pl.BlockSpec(memory_space=pltpu.MemorySpace.HBM)
    chunks = len(keys) // 2
    out_spec, out_shape = acc_spec, jax.ShapeDtypeStruct((4, SPAN, 2 * HEAD_DIM), f32)
    in_specs, args = [q_spec] + [hbm] * len(keys), [q, *keys]
    if acc is None:
        kernel = attn_own_kernel
        scratch = [pltpu.VMEM((2, 4 * SPAN, HEAD_DIM), bf16), pltpu.SemaphoreType.DMA((2,))]
    else:
        in_specs, args = in_specs + [acc_spec], args + [acc]
        kernel = functools.partial(attn_more_kernel, chunks, last, at)
        scratch = [
            pltpu.VMEM((chunks, 2, 4 * SPAN, HEAD_DIM), bf16),
            pltpu.SemaphoreType.DMA((chunks, 2)),
        ]
    if last:
        out_spec = pl.BlockSpec((4, 1, SPAN, HEAD_DIM), lambda i, sc: (0, i, 0, 0))
        out_shape = jax.ShapeDtypeStruct((4, 4, SPAN, HEAD_DIM), bf16)
        scratch = scratch + [pltpu.VMEM((1, SPAN, 2 * HEAD_DIM), f32)]
    return pl.pallas_call(
        kernel,
        out_shape=out_shape,
        grid_spec=pltpu.PrefetchScalarGridSpec(
            num_scalar_prefetch=1,
            grid=(4,),
            in_specs=in_specs,
            out_specs=out_spec,
            scratch_shapes=scratch,
        ),
        cost_estimate=pl.CostEstimate(
            flops=5_000_000_000 * chunks, transcendentals=0, bytes_accessed=4_000_000
        ),
        compiler_params=pltpu.CompilerParams(dimension_semantics=("arbitrary",)),
    )(scalars, *args)


def row_of_sums(m):
    return lax.dot_general(
        jnp.ones((8, m.shape[1]), f32), m, (((1,), (1,)), ((), ())),
        preferred_element_type=f32, precision=lax.Precision.HIGHEST,
    )


def proj_kernel(
    sc_ref, pick_ref, att_ref, w_ref, a1, a2, a3, b1, b2, b3, rp_ref, pg_ref, fg_ref,
    own_ref, zp_ref, abuf, wbuf, asem, wsem,
):
    zi, ci = sc_ref[0], sc_ref[1]
    heads = [zi * 2, zi * 2 + 1]
    heads += [((zi - s + 4) % 4) * 2 + ci for s in (1, 2, 3)]
    heads += [((zi - s + 4) % 4) * 2 + 1 - ci for s in (1, 2, 3)]
    col = pl.multiple_of(zi * COLS, 128)
    src = [w_ref.at[pl.ds(0, 512), pl.ds(col, COLS)], w_ref.at[pl.ds(512, 512), pl.ds(col, COLS)]]
    src += [a1, a2, a3, b1, b2, b3]
    acopies, wcopies = [], []
    for n in range(8):
        acopies.append(
            pltpu.make_async_copy(att_ref.at[pl.ds(heads[n] * 4, 4)], abuf.at[n], asem.at[n])
        )
        wcopies.append(pltpu.make_async_copy(src[n], wbuf.at[n], wsem.at[n]))
        acopies[n].start()
        wcopies[n].start()
    for n in range(8):
        acopies[n].wait()
        wcopies[n].wait()
        lhs = jnp.concatenate([abuf[n, h] for h in range(4)], axis=1)
        part = jnp.dot(lhs, wbuf[n], preferred_element_type=f32)
        if n == 0:
            own_ref[...] = part
        else:
            own_ref[...] += part
    own = own_ref[...]
    squares = row_of_sums(lane_sums(own * own))
    for z in range(4):
        for p in range(PICK):
            zp_ref[z, p : p + 1, :] = own_ref[pl.ds(pick_ref[p], 1), :]
        zp_ref[z, 8:16, :] = rp_ref[...]
        zp_ref[z, 16:17, :] = pg_ref[...]
        zp_ref[z, 17:18, :] = fg_ref[...]
        zp_ref[z, 18:24, :] = jnp.zeros((6, COLS), f32)
        zp_ref[z, 18:19, :LOSS_TOKENS] = squares[:1]


def project(scalars, pick, att, w, parts, res_pick, pg, fg):
    hbm = pl.BlockSpec(memory_space=pltpu.MemorySpace.HBM)
    whole = lambda *dims: pl.BlockSpec(dims, lambda i, *sc: (0,) * len(dims))
    return pl.pallas_call(
        proj_kernel,
        out_shape=(
            jax.ShapeDtypeStruct((BLK, COLS), f32),
            jax.ShapeDtypeStruct((4, 24, COLS), f32),
        ),
        grid_spec=pltpu.PrefetchScalarGridSpec(
            num_scalar_prefetch=2,
            grid=(1,),
            in_specs=[hbm] * 8 + [whole(PICK, COLS), whole(1, COLS), whole(1, COLS)],
            out_specs=(whole(BLK, COLS), whole(4, 24, COLS)),
            scratch_shapes=[
                pltpu.VMEM((8, 4, BLK, HEAD_DIM), bf16),
                pltpu.VMEM((8, 512, COLS), bf16),
                pltpu.SemaphoreType.DMA((8,)),
                pltpu.SemaphoreType.DMA((8,)),
            ],
        ),
        compiler_params=pltpu.CompilerParams(dimension_semantics=("arbitrary",)),
    )(scalars, pick, att, w, *parts, res_pick, pg, fg)


def norm_kernel(zr_ref, ext_ref, out_ref):
    own = [zr_ref[z, :8, :] for z in range(4)]
    total = sum(jnp.sum(o * o, axis=1, keepdims=True) for o in own)
    inv = lax.rsqrt(total / D + epsilon)
    picked = [
        (zr_ref[z, 8:16, :] + own[z] * inv * zr_ref[z, 16:17, :]).astype(bf16).astype(f32)
        for z in range(4)
    ]
    total = sum(jnp.sum(o * o, axis=1, keepdims=True) for o in picked)
    inv = lax.rsqrt(total / D + epsilon)
    for z in range(4):
        normed = (picked[z] * inv * zr_ref[z, 17:18, :]).astype(bf16)
        for n in range(16):
            out_ref[n, :, z * COLS : (z + 1) * COLS] = normed
    for n in range(16):
        out_ref[n, :, D:] = ext_ref[...]


def normalise(zr, ext):
    return pl.pallas_call(
        norm_kernel, out_shape=jax.ShapeDtypeStruct((16, PICK, D + EXT), bf16)
    )(zr, ext)


def loss_kernel(sc_ref, g_ref, s_ref, e_ref, own_ref, sib_ref, row_ref, nbuf, acc, sums):
    j = pl.program_id(0)

    @pl.when(j == 0)
    def _():
        nbuf[:128] = g_ref[...]
        nbuf[128:] = s_ref[...]

    emb = e_ref[...]
    raw = scores(nbuf[:, :D], emb)
    bent = jnp.tanh(raw / logit_cap)
    logits = logit_cap * bent
    big = jnp.exp(logits)
    code = nbuf[:, D:].astype(f32)
    target = code[:, 0:1] * 16384.0 + code[:, 1:2] * 128.0 + code[:, 2:3]
    at = lax.broadcasted_iota(jnp.int32, (LOSS_TOKENS, BLK), 1) + (sc_ref[5] + j * BLK)
    hit = at == target.astype(jnp.int32)
    left = jnp.concatenate(
        [(big * (1.0 - bent * bent)).astype(bf16), jnp.where(hit, 1.0, 0.0).astype(bf16)], axis=0
    )
    both = [lane_sums(big), lane_sums(jnp.where(hit, logits, 0.0))]

    @pl.when(j == 0)
    def _():
        acc[...] = jnp.dot(left, emb, preferred_element_type=f32)
        sums[0], sums[1] = both

    @pl.when(jnp.logical_and(j > 0, j < 3))
    def _():
        acc[...] += jnp.dot(left, emb, preferred_element_type=f32)
        sums[0] += both[0]
        sums[1] += both[1]

    @pl.when(j == 3)
    def _():
        for part in range(2):
            row_ref[part : part + 1] = row_of_sums(sums[part] + both[part])[:1]
        row_ref[2:] = jnp.zeros((6, LOSS_TOKENS), f32)
        for part in range(2):
            for z in range(4):
                cols = slice(z * COLS, (z + 1) * COLS)
                rows = slice(part * 256, (part + 1) * 256)
                whole = acc[rows, cols] + jnp.dot(
                    left[rows], emb[:, cols], preferred_element_type=f32
                )
                lanes = slice(part * COLS, (part + 1) * COLS)
                own_ref[z, :, lanes] = whole[:128].astype(bf16)
                sib_ref[z, :, lanes] = whole[128:].astype(bf16)


def loss_parts(scalars, g, s, emb):
    whole = lambda *dims: pl.BlockSpec(dims, lambda i, sc: (0,) * len(dims))
    return pl.pallas_call(
        loss_kernel,
        out_shape=(
            jax.ShapeDtypeStruct((4, 128, 2 * COLS), bf16),
            jax.ShapeDtypeStruct((4, 128, 2 * COLS), bf16),
            jax.ShapeDtypeStruct((8, LOSS_TOKENS), f32),
        ),
        grid_spec=pltpu.PrefetchScalarGridSpec(
            num_scalar_prefetch=1,
            grid=(4,),
            in_specs=[
                whole(128, D + EXT),
                whole(128, D + EXT),
                pl.BlockSpec((BLK, D), lambda i, sc: (i, 0)),
            ],
            out_specs=(
                whole(4, 128, 2 * COLS), whole(4, 128, 2 * COLS), whole(8, LOSS_TOKENS),
            ),
            scratch_shapes=[
                pltpu.VMEM((LOSS_TOKENS, D + EXT), bf16),
                pltpu.VMEM((2 * LOSS_TOKENS, D), f32),
                pltpu.VMEM((2, LOSS_TOKENS, 128), f32),
            ],
        ),
        compiler_params=pltpu.CompilerParams(dimension_semantics=("arbitrary",)),
    )(scalars, g, s, emb)


def join_kernel(own_ref, sib_ref, info_ref, out_ref):
    out_ref[0, :, : 2 * COLS] = (own_ref[0].astype(f32) + sib_ref[0].astype(f32)).astype(bf16)
    for n in range(16):
        out_ref[0, n * 8 : (n + 1) * 8, 2 * COLS :] = info_ref[...].astype(bf16)


def join(own, sib, info):
    block = pl.BlockSpec((1, 128, 2 * COLS), lambda z: (z, 0, 0))
    return pl.pallas_call(
        join_kernel,
        out_shape=jax.ShapeDtypeStruct((4, 128, 2 * COLS + EXT), bf16),
        grid=(4,),
        in_specs=[block, block, pl.BlockSpec((8, EXT), lambda z: (0, 0))],
        out_specs=pl.BlockSpec((1, 128, 2 * COLS + EXT), lambda z: (z, 0, 0)),
    )(own, sib, info)


def shards(
    query_rows, key_rows, value_rows, residual, out_weight, post_gain, final_gain,
    embedding, targets, loss_mask, pick_pos,
):
    xi, yi, ci, zi = (lax.axis_index(a) for a in ("x", "y", "core", "vocab"))
    base = (((xi * 4 + yi) * 2 + ci) * 4 + zi) * embedding.shape[0]
    scalars = jnp.stack(
        [zi, ci, jnp.where(yi >= 1, 0, 1), jnp.where(yi == 3, 0, 1), jnp.where(yi >= 2, 0, 1), base]
    ).astype(jnp.int32)

    q_heads = query_rows.reshape(BLK, 8, HEAD_DIM).transpose(1, 0, 2)
    k_heads = key_rows.reshape(BLK, 4, HEAD_DIM).transpose(1, 0, 2)
    v_heads = value_rows.reshape(BLK, 4, HEAD_DIM).transpose(1, 0, 2)
    kv = jnp.stack([k_heads, v_heads], axis=1).reshape(8, BLK, HEAD_DIM)
    got = exchange(jnp.concatenate([q_heads, kv], axis=1), ("x", "core"))
    q = got[:, :BLK].reshape(4, SPAN, HEAD_DIM)
    own = got[:, BLK:].reshape(4 * SPAN, HEAD_DIM)

    swap = lambda a: lax.ppermute(a, "core", SWAP)
    own_pair = [own, swap(own)]
    got_y = []
    for k in (1, 3, 2):
        got_y.append(lax.ppermute(own, "y", ring(k)))
    down, up, far = got_y

    mine = []
    for s in (1, 2, 3):
        part = lax.dynamic_slice(out_weight, (ci * 512, ((zi + s) % 4) * COLS), (512, COLS))
        mine.append(lax.ppermute(part, "vocab", ring(s)))
    theirs = [swap(p) for p in mine]

    acc = attn_call(scalars, q, own_pair)
    acc = attn_call(scalars, q, [down, swap(down)], acc, at=2)
    out = attn_call(scalars, q, [up, swap(up), far, swap(far)], acc, at=3, last=True)
    att = exchange(out.reshape(32, BLK, HEAD_DIM), ("vocab", "x", "core"))

    res_pick = jnp.take(residual, pick_pos, axis=0).astype(f32)
    own_cols, zp = project(
        scalars, pick_pos, att, out_weight, mine + theirs,
        res_pick, post_gain[None], final_gain[None],
    )
    zr = exchange(zp, "vocab")
    square_sum = jnp.sum(zr[:, 18, :LOSS_TOKENS], axis=0)
    inv_rms = lax.rsqrt(square_sum / D + epsilon)[:, None]
    final_hidden = (residual.astype(f32) + own_cols * inv_rms * post_gain).astype(bf16)

    coded = jnp.stack([targets >> 14, (targets >> 7) & 127, targets & 127, loss_mask], axis=1)
    ext = jnp.pad(coded, ((0, 0), (0, EXT - 4))).astype(bf16)
    g = exchange(normalise(zr, ext), ("x", "y")).reshape(128, D + EXT)
    own_part, sib_part, rows = loss_parts(scalars, g, swap(g), embedding)

    row = rows[:2, :128] + swap(rows[:2, 128:])
    high = lax.reduce_precision(row, 8, 7)
    low = row - high
    info = jnp.stack([high[0], low[0], high[1], low[1]] + [jnp.zeros((128,), f32)] * 4)
    payload = join(own_part, swap(sib_part), info).reshape(64, 8, 2 * COLS + EXT)
    back = exchange(payload, ("vocab", "x", "y"))
    facts = jnp.sum(back[:, :4, 2 * COLS :].astype(f32), axis=0)
    totals, target_logit = facts[0] + facts[1], facts[2] + facts[3]
    masks = g[:, D + 3].astype(f32)
    loss = jnp.sum(masks * (jnp.log(totals) - target_logit)) / LOSS_TOKENS
    loss = loss + lax.ppermute(loss[None], "core", SWAP)[0]

    sums = jnp.sum(back[:, :, : 2 * COLS].astype(f32), axis=0)
    at = (xi * 4 + yi) * PICK
    my_total = lax.dynamic_slice(totals, (at,), (PICK,))[:, None]
    my_logit = lax.dynamic_slice(target_logit, (at,), (PICK,))[:, None]
    slope = 1.0 - (my_logit / logit_cap) ** 2
    grad = loss_mask.astype(f32)[:, None] * (sums[:, :COLS] / my_total - slope * sums[:, COLS:])
    return (final_hidden, loss, grad)


def solution(mesh):
    split = Mesh(
        mesh.devices.reshape(4, 4, 2, mesh.shape["vocab"]), ("x", "y", "core", "vocab")
    )

    return jax.shard_map(
        shards,
        mesh=split,
        in_specs=(
            P(CTX, "vocab"),
            P(CTX, "vocab"),
            P(CTX, "vocab"),
            P(CTX, "vocab"),
            P("vocab", None),
            P("vocab"),
            P("vocab"),
            P((*CTX, "vocab"), None),
            P(CTX),
            P(CTX),
            P(CTX),
        ),
        out_specs=(P(CTX, "vocab"), P(), P(CTX, "vocab")),
        check_vma=False,
    )
```

```python
import functools

import jax
import jax.numpy as jnp
from jax import lax
from jax.experimental import pallas as pl
from jax.experimental.pallas import tpu as pltpu
from jax.sharding import Mesh
from jax.sharding import PartitionSpec as P


D = 4608
HEAD_DIM = 128
PICK = 8
SPAN = 512
BLK = 256
COLS = 1152
EXT = 128
LOSS_TOKENS = 256
CTX = ("x", "y", "core")

attn_cap = 50.0
logit_cap = 30.0
query_scalar = 144.0
epsilon = 1e-06

f32 = jnp.float32
bf16 = jnp.bfloat16


def ring(k):
    return [(j, (j + k) % 4) for j in range(4)]


SWAP = [(0, 1), (1, 0)]


def in_vmem(a):
    return pltpu.with_memory_space_constraint(a, pltpu.MemorySpace.VMEM)


def params(mib):
    return pltpu.CompilerParams(
        dimension_semantics=("arbitrary",), vmem_limit_bytes=mib * 1024 * 1024
    )


VMEM_SPEC = pl.BlockSpec(memory_space=pltpu.MemorySpace.VMEM)


def pack_kernel(q_ref, k_ref, v_ref, out_ref):
    for h, other in enumerate((k_ref, v_ref)):
        out_ref[h, :BLK, :] = q_ref[:, h * HEAD_DIM : (h + 1) * HEAD_DIM]
        out_ref[h, BLK:, :] = other[...]


def pack(q, k, v):
    one = pl.BlockSpec((BLK, HEAD_DIM), lambda i: (0, i))
    return pl.pallas_call(
        pack_kernel,
        out_shape=jax.ShapeDtypeStruct((8, SPAN, HEAD_DIM), bf16),
        grid=(4,),
        in_specs=[pl.BlockSpec((BLK, 2 * HEAD_DIM), lambda i: (0, i)), one, one],
        out_specs=pl.BlockSpec((2, SPAN, HEAD_DIM), lambda i: (i, 0, 0)),
        compiler_params=params(16),
    )(q, k, v)


def exchange(pieces, axes):
    return lax.all_to_all(pieces, axes, 0, 0, tiled=True)


def scores(q, k):
    return lax.dot_general(q, k, (((1,), (1,)), ((), ())), preferred_element_type=f32)


def weigh(raw):
    return jnp.exp(attn_cap * jnp.tanh(raw * (query_scalar**-0.5 / attn_cap)))


def lane_sums(p):
    parts = [p[:, i : i + 128] for i in range(0, p.shape[1], 128)]
    return functools.reduce(jnp.add, parts)


def load_kv(core, a_ref, b_ref, buf, sem):
    copies = [
        pltpu.make_async_copy(a_ref, buf.at[core], sem.at[0]),
        pltpu.make_async_copy(b_ref, buf.at[1 - core], sem.at[1]),
    ]
    for copy in copies:
        copy.start()
    return copies


def in_turn(tasks):
    results = []
    raw = tasks[0][0]()
    for n, (_, after) in enumerate(tasks):
        ahead = tasks[n + 1][0]() if n + 1 < len(tasks) else None
        results.append(after(weigh(raw)))
        raw = ahead
    return results


def times_values(p, v):
    return jnp.dot(p.astype(bf16), v, preferred_element_type=f32), lane_sums(p)


def seen(q, buf, first, span, valid=None):
    def before():
        return scores(q, buf[0, pl.ds(first, span), :])

    def after(p):
        if valid is not None:
            p = jnp.where(valid, p, 0.0)
        return times_values(p, buf[1, pl.ds(first, span), :])

    return before, after


def attn_own_kernel(sc_ref, q_ref, a_ref, b_ref, acc_ref, buf, sem):
    i = pl.program_id(0)

    @pl.when(i == 0)
    def _():
        for copy in load_kv(sc_ref[1], a_ref, b_ref, buf, sem):
            copy.wait()

    def body(earlier):
        has_edge = i >= 2
        edge0 = jnp.maximum(i - 2, 0) * SPAN
        diag0 = i * SPAN
        tq = lax.broadcasted_iota(jnp.int32, (BLK, BLK), 0)
        tk = lax.broadcasted_iota(jnp.int32, (BLK, BLK), 1)
        causal = tk <= tq
        beyond = jnp.logical_and(jnp.logical_not(causal), has_edge)
        q = [q_ref[0, pl.ds(r * BLK, BLK), :] for r in range(2)]

        def corner(r):
            def before():
                raw = scores(q[r], buf[0, pl.ds(diag0 + r * BLK, BLK), :])
                if earlier:
                    edge = scores(q[r], buf[0, pl.ds(edge0 + r * BLK, BLK), :])
                    raw = jnp.where(causal, raw, edge)
                return raw

            def after(p):
                pd = jnp.where(causal, p, 0.0)
                top, low = times_values(pd, buf[1, pl.ds(diag0 + r * BLK, BLK), :])
                if earlier:
                    pe = jnp.where(beyond, p, 0.0)
                    more = times_values(pe, buf[1, pl.ds(edge0 + r * BLK, BLK), :])
                    top, low = top + more[0], low + more[1]
                return top, low

            return before, after

        tasks = [corner(0), corner(1), seen(q[1], buf, diag0, BLK)]
        if earlier:
            tasks.append(seen(q[0], buf, edge0 + BLK, BLK, has_edge))
            tasks.append(seen(q_ref[0], buf, (i - 1) * SPAN, SPAN))
        parts = in_turn(tasks)
        for r in range(2):
            for lane in range(2):
                total = parts[r][lane]
                if r == 1:
                    total += parts[2][lane]
                if earlier and r == 0:
                    total += parts[3][lane]
                if earlier:
                    total += parts[4][lane][r * BLK : (r + 1) * BLK]
                acc_ref[0, pl.ds(r * BLK, BLK), lane * HEAD_DIM : (lane + 1) * HEAD_DIM] = total

    pl.when(i == 0)(lambda: body(False))
    pl.when(i > 0)(lambda: body(True))


def attn_more_kernel(chunks, last, at, sc_ref, q_ref, *refs):
    keys, (in_ref, out_ref, buf, sem, *scr) = refs[: 2 * chunks], refs[2 * chunks :]
    i = pl.program_id(0)
    acc_ref = scr[0] if last else out_ref

    @pl.when(i == 0)
    def _():
        copies = []
        for n in range(chunks):
            copies += load_kv(sc_ref[1], keys[2 * n], keys[2 * n + 1], buf.at[n], sem.at[n])
        for copy in copies:
            copy.wait()
        acc_ref[...] = in_ref[...]

    def add(base, tasks):
        for lane, lanes in enumerate((slice(0, HEAD_DIM), slice(HEAD_DIM, 2 * HEAD_DIM))):
            if lane == 0:
                parts = in_turn(tasks)
            total = base[0, :, lanes]
            for part in parts:
                total += part[lane]
            acc_ref[0, :, lanes] = total

    for n in range(chunks):

        @pl.when(jnp.logical_and(i == 0, sc_ref[at + n] == 0))
        def _():
            add(acc_ref, [seen(q_ref[0], buf.at[n], 0, SPAN)])

    @pl.when(i > 0)
    def _():
        tasks = []
        for n in range(chunks):
            newest = i - sc_ref[at + n]
            first = jnp.maximum(newest - 1, 0) * SPAN
            tasks.append(seen(q_ref[0], buf.at[n], first, SPAN))
            tasks.append(seen(q_ref[0], buf.at[n], first + SPAN, SPAN, newest > 0))
        add(in_ref, tasks)

    if last:
        whole = jnp.sum(acc_ref[0, :, HEAD_DIM:], axis=1, keepdims=True)
        done = (acc_ref[0, :, :HEAD_DIM] / whole).astype(bf16)
        for z in range(4):
            out_ref[z, 0] = done


def attn_call(scalars, q, keys, acc=None, at=0, last=False):
    q_spec = pl.BlockSpec((1, SPAN, HEAD_DIM), lambda i, sc: (i, 0, 0))
    acc_spec = pl.BlockSpec((1, SPAN, 2 * HEAD_DIM), lambda i, sc: (i, 0, 0))
    hbm = pl.BlockSpec(memory_space=pltpu.MemorySpace.HBM)
    chunks = len(keys) // 2
    out_spec, out_shape = acc_spec, jax.ShapeDtypeStruct((4, SPAN, 2 * HEAD_DIM), f32)
    in_specs, args = [q_spec] + [hbm] * len(keys), [q, *keys]
    if acc is None:
        kernel = attn_own_kernel
        scratch = [pltpu.VMEM((2, 4 * SPAN, HEAD_DIM), bf16), pltpu.SemaphoreType.DMA((2,))]
    else:
        in_specs, args = in_specs + [acc_spec], args + [acc]
        kernel = functools.partial(attn_more_kernel, chunks, last, at)
        scratch = [
            pltpu.VMEM((chunks, 2, 4 * SPAN, HEAD_DIM), bf16),
            pltpu.SemaphoreType.DMA((chunks, 2)),
        ]
    if last:
        out_spec = pl.BlockSpec((4, 1, SPAN, HEAD_DIM), lambda i, sc: (0, i, 0, 0))
        out_shape = pltpu.MemorySpace.HBM((4, 4, SPAN, HEAD_DIM), bf16)
        scratch = scratch + [pltpu.VMEM((1, SPAN, 2 * HEAD_DIM), f32)]
    return pl.pallas_call(
        kernel,
        out_shape=out_shape,
        grid_spec=pltpu.PrefetchScalarGridSpec(
            num_scalar_prefetch=1,
            grid=(4,),
            in_specs=in_specs,
            out_specs=out_spec,
            scratch_shapes=scratch,
        ),
        cost_estimate=pl.CostEstimate(
            flops=5_000_000_000 * chunks, transcendentals=0, bytes_accessed=4_000_000
        ),
        compiler_params=params(20),
    )(scalars, *args)


def row_of_sums(m):
    return lax.dot_general(
        jnp.ones((8, m.shape[1]), f32), m, (((1,), (1,)), ((), ())),
        preferred_element_type=f32, precision=lax.Precision.HIGHEST,
    )


def proj_kernel(
    sc_ref, pick_ref, att_ref, w_ref, a1, a2, a3, b1, b2, b3, rp_ref, pg_ref, fg_ref,
    own_ref, zp_ref,
):
    zi, ci = sc_ref[0], sc_ref[1]
    heads = [zi * 2, zi * 2 + 1]
    heads += [((zi - s + 4) % 4) * 2 + ci for s in (1, 2, 3)]
    heads += [((zi - s + 4) % 4) * 2 + 1 - ci for s in (1, 2, 3)]
    weights = [w_ref.at[:512], w_ref.at[512:], a1, a2, a3, b1, b2, b3]
    total = None
    for n in range(8):
        lhs = jnp.concatenate([att_ref[heads[n] * 4 + h] for h in range(4)], axis=1)
        part = jnp.dot(lhs, weights[n][...], preferred_element_type=f32)
        total = part if total is None else total + part
    own_ref[...] = total
    own = own_ref[...]
    squares = row_of_sums(lane_sums(own * own))
    for z in range(4):
        for p in range(PICK):
            zp_ref[z, p : p + 1, :] = own_ref[pl.ds(pick_ref[p], 1), :]
        zp_ref[z, 8:16, :] = rp_ref[...]
        zp_ref[z, 16:17, :] = pg_ref[...]
        zp_ref[z, 17:18, :] = fg_ref[...]
        zp_ref[z, 18:24, :] = jnp.zeros((6, COLS), f32)
        zp_ref[z, 18:19, :LOSS_TOKENS] = squares[:1]


def project(scalars, pick, att, w, parts, res_pick, pg, fg):
    whole = lambda *dims: pl.BlockSpec(dims, lambda i, *sc: (0,) * len(dims))
    return pl.pallas_call(
        proj_kernel,
        out_shape=(
            pltpu.MemorySpace.HBM((BLK, COLS), f32),
            pltpu.MemorySpace.HBM((4, 24, COLS), f32),
        ),
        grid_spec=pltpu.PrefetchScalarGridSpec(
            num_scalar_prefetch=2,
            grid=(1,),
            in_specs=[VMEM_SPEC] * 8
            + [whole(PICK, COLS), whole(1, COLS), whole(1, COLS)],
            out_specs=(whole(BLK, COLS), whole(4, 24, COLS)),
        ),
        compiler_params=params(20),
    )(scalars, pick, in_vmem(att), in_vmem(w), *[in_vmem(p) for p in parts], res_pick, pg, fg)


def norm_kernel(zr_ref, ext_ref, out_ref):
    own = [zr_ref[z, :8, :] for z in range(4)]
    total = sum(jnp.sum(o * o, axis=1, keepdims=True) for o in own)
    inv = lax.rsqrt(total / D + epsilon)
    picked = [
        (zr_ref[z, 8:16, :] + own[z] * inv * zr_ref[z, 16:17, :]).astype(bf16).astype(f32)
        for z in range(4)
    ]
    total = sum(jnp.sum(o * o, axis=1, keepdims=True) for o in picked)
    inv = lax.rsqrt(total / D + epsilon)
    for z in range(4):
        normed = (picked[z] * inv * zr_ref[z, 17:18, :]).astype(bf16)
        for n in range(16):
            out_ref[n, :, z * COLS : (z + 1) * COLS] = normed
    for n in range(16):
        out_ref[n, :, D:] = ext_ref[...]


def normalise(zr, ext):
    return pl.pallas_call(
        norm_kernel,
        out_shape=jax.ShapeDtypeStruct((16, PICK, D + EXT), bf16),
        in_specs=[VMEM_SPEC, pl.BlockSpec((PICK, EXT), lambda: (0, 0))],
        compiler_params=pltpu.CompilerParams(vmem_limit_bytes=16 * 1024 * 1024),
    )(in_vmem(zr), ext)


def loss_kernel(sc_ref, g_ref, s_ref, e_ref, own_ref, sib_ref, nbuf, acc, sums):
    j = pl.program_id(0)

    @pl.when(j == 0)
    def _():
        nbuf[:128] = g_ref[...]
        nbuf[128:] = s_ref[...]

    emb = e_ref[...]
    raw = scores(nbuf[:, :D], emb)
    bent = jnp.tanh(raw / logit_cap)
    logits = logit_cap * bent
    big = jnp.exp(logits)
    code = nbuf[:, D:].astype(f32)
    target = code[:, 0:1] * 16384.0 + code[:, 1:2] * 128.0 + code[:, 2:3]
    at = lax.broadcasted_iota(jnp.int32, (LOSS_TOKENS, BLK), 1) + (sc_ref[5] + j * BLK)
    hit = at == target.astype(jnp.int32)
    left = jnp.concatenate(
        [(big * (1.0 - bent * bent)).astype(bf16), jnp.where(hit, 1.0, 0.0).astype(bf16)], axis=0
    )
    both = [lane_sums(big), lane_sums(jnp.where(hit, logits, 0.0))]

    @pl.when(j == 0)
    def _():
        acc[...] = jnp.dot(left, emb, preferred_element_type=f32)
        sums[0], sums[1] = both

    @pl.when(jnp.logical_and(j > 0, j < 3))
    def _():
        acc[...] += jnp.dot(left, emb, preferred_element_type=f32)
        sums[0] += both[0]
        sums[1] += both[1]

    @pl.when(j == 3)
    def _():
        facts = []
        for part in range(2):
            row = row_of_sums(sums[part] + both[part])[:1]
            high = row.astype(bf16).astype(f32)
            facts += [high, row - high]
        none = jnp.zeros((4, 128), f32)
        mine = jnp.concatenate([r[:, :128] for r in facts] + [none], axis=0)
        theirs = jnp.concatenate([none] + [r[:, 128:] for r in facts], axis=0)
        for ref, info in ((own_ref, mine), (sib_ref, theirs)):
            tall = jnp.concatenate([info] * 16, axis=0).astype(bf16)
            for z in range(4):
                ref[z, :, 2 * COLS :] = tall
        for part in range(2):
            for z in range(4):
                cols = slice(z * COLS, (z + 1) * COLS)
                rows = slice(part * 256, (part + 1) * 256)
                whole = acc[rows, cols] + jnp.dot(
                    left[rows], emb[:, cols], preferred_element_type=f32
                )
                lanes = slice(part * COLS, (part + 1) * COLS)
                own_ref[z, :, lanes] = whole[:128].astype(bf16)
                sib_ref[z, :, lanes] = whole[128:].astype(bf16)


def loss_parts(scalars, g, s, emb):
    whole = lambda *dims: pl.BlockSpec(dims, lambda i, sc: (0,) * len(dims))
    return pl.pallas_call(
        loss_kernel,
        out_shape=(
            jax.ShapeDtypeStruct((4, 128, 2 * COLS + EXT), bf16),
            jax.ShapeDtypeStruct((4, 128, 2 * COLS + EXT), bf16),
        ),
        grid_spec=pltpu.PrefetchScalarGridSpec(
            num_scalar_prefetch=1,
            grid=(4,),
            in_specs=[
                VMEM_SPEC,
                VMEM_SPEC,
                pl.BlockSpec((BLK, D), lambda i, sc: (i, 0)),
            ],
            out_specs=(whole(4, 128, 2 * COLS + EXT), whole(4, 128, 2 * COLS + EXT)),
            scratch_shapes=[
                pltpu.VMEM((LOSS_TOKENS, D + EXT), bf16),
                pltpu.VMEM((2 * LOSS_TOKENS, D), f32),
                pltpu.VMEM((2, LOSS_TOKENS, 128), f32),
            ],
        ),
        compiler_params=params(44),
    )(scalars, in_vmem(g), in_vmem(s), emb)


def shards(
    query_rows, key_rows, value_rows, residual, out_weight, post_gain, final_gain,
    embedding, targets, loss_mask, pick_pos,
):
    xi, yi, ci, zi = (lax.axis_index(a) for a in ("x", "y", "core", "vocab"))
    base = (((xi * 4 + yi) * 2 + ci) * 4 + zi) * embedding.shape[0]
    scalars = jnp.stack(
        [zi, ci, jnp.where(yi >= 1, 0, 1), jnp.where(yi == 3, 0, 1), jnp.where(yi >= 2, 0, 1), base]
    ).astype(jnp.int32)

    packed = pack(query_rows, key_rows, value_rows)
    got = exchange(packed, ("x", "core"))
    q = got[:, :BLK].reshape(4, SPAN, HEAD_DIM)
    own = got[:, BLK:].reshape(4 * SPAN, HEAD_DIM)

    swap = lambda a: lax.ppermute(a, "core", SWAP)
    own_pair = [own, swap(own)]
    got_y = []
    for k in (1, 3, 2):
        got_y.append(lax.ppermute(own, "y", ring(k)))
    down, up, far = got_y

    mine = []
    for s in (1, 2, 3):
        part = lax.dynamic_slice(out_weight, (ci * 512, ((zi + s) % 4) * COLS), (512, COLS))
        mine.append(lax.ppermute(part, "vocab", ring(s)))
    theirs = [swap(p) for p in mine]

    acc = attn_call(scalars, q, own_pair)
    acc = attn_call(scalars, q, [down, swap(down)], acc, at=2)
    out = attn_call(scalars, q, [up, swap(up), far, swap(far)], acc, at=3, last=True)
    att = exchange(out.reshape(32, BLK, HEAD_DIM), ("vocab", "x", "core"))
    kept = lax.dynamic_slice(out_weight, (0, zi * COLS), (1024, COLS))

    res_pick = jnp.take(residual, pick_pos, axis=0).astype(f32)
    own_cols, zp = project(
        scalars, pick_pos, att, kept, mine + theirs,
        res_pick, post_gain[None], final_gain[None],
    )
    zr = exchange(zp, "vocab")
    square_sum = jnp.sum(zr[:, 18, :LOSS_TOKENS], axis=0)
    inv_rms = lax.rsqrt(square_sum / D + epsilon)[:, None]
    final_hidden = (residual.astype(f32) + own_cols * inv_rms * post_gain).astype(bf16)

    coded = jnp.stack([targets >> 14, (targets >> 7) & 127, targets & 127, loss_mask], axis=1)
    ext = jnp.pad(coded, ((0, 0), (0, EXT - 4))).astype(bf16)
    normed = normalise(zr, ext)
    g = exchange(normed, ("x", "y")).reshape(128, D + EXT)
    own_part, sib_part = loss_parts(scalars, g, swap(g), embedding)
    payload = (own_part.astype(f32) + swap(sib_part).astype(f32)).astype(bf16)
    back = exchange(payload.reshape(64, 8, 2 * COLS + EXT), ("vocab", "x", "y"))
    facts = jnp.sum(back[:, :, 2 * COLS :].astype(f32), axis=0)
    totals = facts[0] + facts[1] + facts[4] + facts[5]
    target_logit = facts[2] + facts[3] + facts[6] + facts[7]
    masks = g[:, D + 3].astype(f32)
    loss = jnp.sum(masks * (jnp.log(totals) - target_logit)) / LOSS_TOKENS
    loss = loss + lax.ppermute(loss[None], "core", SWAP)[0]

    sums = jnp.sum(back[:, :, : 2 * COLS].astype(f32), axis=0)
    at = (xi * 4 + yi) * PICK
    my_total = lax.dynamic_slice(totals, (at,), (PICK,))[:, None]
    my_logit = lax.dynamic_slice(target_logit, (at,), (PICK,))[:, None]
    slope = 1.0 - (my_logit / logit_cap) ** 2
    grad = loss_mask.astype(f32)[:, None] * (sums[:, :COLS] / my_total - slope * sums[:, COLS:])
    return (final_hidden, loss, grad)


def solution(mesh):
    split = Mesh(
        mesh.devices.reshape(4, 4, 2, mesh.shape["vocab"]), ("x", "y", "core", "vocab")
    )

    return jax.shard_map(
        shards,
        mesh=split,
        in_specs=(
            P(CTX, "vocab"),
            P(CTX, "vocab"),
            P(CTX, "vocab"),
            P(CTX, "vocab"),
            P("vocab", None),
            P("vocab"),
            P("vocab"),
            P((*CTX, "vocab"), None),
            P(CTX),
            P(CTX),
            P(CTX),
        ),
        out_specs=(P(CTX, "vocab"), P(), P(CTX, "vocab")),
        check_vma=False,
    )
```

```python
import functools

import jax
import jax.numpy as jnp
from jax import lax
from jax.experimental import pallas as pl
from jax.experimental.pallas import tpu as pltpu
from jax.sharding import Mesh
from jax.sharding import PartitionSpec as P


D = 4608
HEAD_DIM = 128
PICK = 8
SPAN = 512
BLK = 256
COLS = 1152
EXT = 128
WIDE = 2 * COLS + 2 * EXT
LOSS_TOKENS = 256
CTX = ("x", "y", "core")

attn_cap = 50.0
logit_cap = 30.0
query_scalar = 144.0
epsilon = 1e-06

f32 = jnp.float32
bf16 = jnp.bfloat16


def ring(k):
    return [(j, (j + k) % 4) for j in range(4)]


SWAP = [(0, 1), (1, 0)]


def in_vmem(a):
    return pltpu.with_memory_space_constraint(a, pltpu.MemorySpace.VMEM)


def params(mib):
    return pltpu.CompilerParams(
        dimension_semantics=("arbitrary",), vmem_limit_bytes=mib * 1024 * 1024
    )


VMEM_SPEC = pl.BlockSpec(memory_space=pltpu.MemorySpace.VMEM)


def pack_kernel(q_ref, k_ref, v_ref, out_ref):
    for h, other in enumerate((k_ref, v_ref)):
        out_ref[h, :BLK, :] = q_ref[:, h * HEAD_DIM : (h + 1) * HEAD_DIM]
        out_ref[h, BLK:, :] = other[...]


def pack(q, k, v):
    one = pl.BlockSpec((BLK, HEAD_DIM), lambda i: (0, i))
    return pl.pallas_call(
        pack_kernel,
        out_shape=jax.ShapeDtypeStruct((8, SPAN, HEAD_DIM), bf16),
        grid=(4,),
        in_specs=[pl.BlockSpec((BLK, 2 * HEAD_DIM), lambda i: (0, i)), one, one],
        out_specs=pl.BlockSpec((2, SPAN, HEAD_DIM), lambda i: (i, 0, 0)),
    )(q, k, v)


def exchange(pieces, axes):
    return lax.all_to_all(pieces, axes, 0, 0, tiled=True)


def scores(q, k):
    return lax.dot_general(q, k, (((1,), (1,)), ((), ())), preferred_element_type=f32)


def weigh(raw):
    return jnp.exp(attn_cap * jnp.tanh(raw * (query_scalar**-0.5 / attn_cap)))


def lane_sums(p):
    parts = [p[:, i : i + 128] for i in range(0, p.shape[1], 128)]
    return functools.reduce(jnp.add, parts)


def load_kv(core, a_ref, b_ref, buf, sem):
    copies = [
        pltpu.make_async_copy(a_ref, buf.at[core], sem.at[0]),
        pltpu.make_async_copy(b_ref, buf.at[1 - core], sem.at[1]),
    ]
    for copy in copies:
        copy.start()
    return copies


def in_turn(tasks):
    results = []
    raw = tasks[0][0]()
    for n, (_, after) in enumerate(tasks):
        ahead = tasks[n + 1][0]() if n + 1 < len(tasks) else None
        results.append(after(weigh(raw)))
        raw = ahead
    return results


def times_values(p, v):
    return jnp.dot(p.astype(bf16), v, preferred_element_type=f32), lane_sums(p)


def seen(q, buf, first, span, valid=None):
    def before():
        return scores(q, buf[0, pl.ds(first, span), :])

    def after(p):
        if valid is not None:
            p = jnp.where(valid, p, 0.0)
        return times_values(p, buf[1, pl.ds(first, span), :])

    return before, after


def attn_own_kernel(sc_ref, q_ref, a_ref, b_ref, acc_ref, buf, sem):
    i = pl.program_id(0)

    @pl.when(i == 0)
    def _():
        for copy in load_kv(sc_ref[1], a_ref, b_ref, buf, sem):
            copy.wait()

    def body(earlier):
        has_edge = i >= 2
        edge0 = jnp.maximum(i - 2, 0) * SPAN
        diag0 = i * SPAN
        tq = lax.broadcasted_iota(jnp.int32, (BLK, BLK), 0)
        tk = lax.broadcasted_iota(jnp.int32, (BLK, BLK), 1)
        causal = tk <= tq
        beyond = jnp.logical_and(jnp.logical_not(causal), has_edge)
        q = [q_ref[0, pl.ds(r * BLK, BLK), :] for r in range(2)]

        def corner(r):
            def before():
                raw = scores(q[r], buf[0, pl.ds(diag0 + r * BLK, BLK), :])
                if earlier:
                    edge = scores(q[r], buf[0, pl.ds(edge0 + r * BLK, BLK), :])
                    raw = jnp.where(causal, raw, edge)
                return raw

            def after(p):
                pd = jnp.where(causal, p, 0.0)
                top, low = times_values(pd, buf[1, pl.ds(diag0 + r * BLK, BLK), :])
                if earlier:
                    pe = jnp.where(beyond, p, 0.0)
                    more = times_values(pe, buf[1, pl.ds(edge0 + r * BLK, BLK), :])
                    top, low = top + more[0], low + more[1]
                return top, low

            return before, after

        tasks = [corner(0), corner(1), seen(q[1], buf, diag0, BLK)]
        if earlier:
            tasks.append(seen(q[0], buf, edge0 + BLK, BLK, has_edge))
            tasks.append(seen(q_ref[0], buf, (i - 1) * SPAN, SPAN))
        parts = in_turn(tasks)
        for r in range(2):
            for lane in range(2):
                total = parts[r][lane]
                if r == 1:
                    total += parts[2][lane]
                if earlier and r == 0:
                    total += parts[3][lane]
                if earlier:
                    total += parts[4][lane][r * BLK : (r + 1) * BLK]
                acc_ref[0, pl.ds(r * BLK, BLK), lane * HEAD_DIM : (lane + 1) * HEAD_DIM] = total

    pl.when(i == 0)(lambda: body(False))
    pl.when(i > 0)(lambda: body(True))


def attn_more_kernel(chunks, last, at, sc_ref, q_ref, *refs):
    keys, (in_ref, out_ref, buf, sem, *scr) = refs[: 2 * chunks], refs[2 * chunks :]
    i = pl.program_id(0)
    acc_ref = scr[0] if last else out_ref

    @pl.when(i == 0)
    def _():
        copies = []
        for n in range(chunks):
            copies += load_kv(sc_ref[1], keys[2 * n], keys[2 * n + 1], buf.at[n], sem.at[n])
        for copy in copies:
            copy.wait()
        acc_ref[...] = in_ref[...]

    def add(base, tasks):
        for lane, lanes in enumerate((slice(0, HEAD_DIM), slice(HEAD_DIM, 2 * HEAD_DIM))):
            if lane == 0:
                parts = in_turn(tasks)
            total = base[0, :, lanes]
            for part in parts:
                total += part[lane]
            acc_ref[0, :, lanes] = total

    for n in range(chunks):

        @pl.when(jnp.logical_and(i == 0, sc_ref[at + n] == 0))
        def _():
            add(acc_ref, [seen(q_ref[0], buf.at[n], 0, SPAN)])

    @pl.when(i > 0)
    def _():
        tasks = []
        for n in range(chunks):
            newest = i - sc_ref[at + n]
            first = jnp.maximum(newest - 1, 0) * SPAN
            tasks.append(seen(q_ref[0], buf.at[n], first, SPAN))
            tasks.append(seen(q_ref[0], buf.at[n], first + SPAN, SPAN, newest > 0))
        add(in_ref, tasks)

    if last:
        whole = jnp.sum(acc_ref[0, :, HEAD_DIM:], axis=1, keepdims=True)
        done = (acc_ref[0, :, :HEAD_DIM] / whole).astype(bf16)
        for z in range(4):
            out_ref[z, 0] = done


def attn_call(scalars, q, keys, acc=None, at=0, last=False):
    q_spec = pl.BlockSpec((1, SPAN, HEAD_DIM), lambda i, sc: (i, 0, 0))
    acc_spec = pl.BlockSpec((1, SPAN, 2 * HEAD_DIM), lambda i, sc: (i, 0, 0))
    hbm = pl.BlockSpec(memory_space=pltpu.MemorySpace.HBM)
    chunks = len(keys) // 2
    out_spec, out_shape = acc_spec, jax.ShapeDtypeStruct((4, SPAN, 2 * HEAD_DIM), f32)
    in_specs, args = [q_spec] + [hbm] * len(keys), [q, *keys]
    if acc is None:
        kernel = attn_own_kernel
        scratch = [pltpu.VMEM((2, 4 * SPAN, HEAD_DIM), bf16), pltpu.SemaphoreType.DMA((2,))]
    else:
        in_specs, args = in_specs + [acc_spec], args + [acc]
        kernel = functools.partial(attn_more_kernel, chunks, last, at)
        scratch = [
            pltpu.VMEM((chunks, 2, 4 * SPAN, HEAD_DIM), bf16),
            pltpu.SemaphoreType.DMA((chunks, 2)),
        ]
    if last:
        out_spec = pl.BlockSpec((4, 1, SPAN, HEAD_DIM), lambda i, sc: (0, i, 0, 0))
        out_shape = pltpu.MemorySpace.HBM((4, 4, SPAN, HEAD_DIM), bf16)
        scratch = scratch + [pltpu.VMEM((1, SPAN, 2 * HEAD_DIM), f32)]
    return pl.pallas_call(
        kernel,
        out_shape=out_shape,
        grid_spec=pltpu.PrefetchScalarGridSpec(
            num_scalar_prefetch=1,
            grid=(4,),
            in_specs=in_specs,
            out_specs=out_spec,
            scratch_shapes=scratch,
        ),
        cost_estimate=pl.CostEstimate(
            flops=5_000_000_000 * chunks, transcendentals=0, bytes_accessed=4_000_000
        ),
        compiler_params=params(20),
    )(scalars, *args)


def row_of_sums(m):
    return lax.dot_general(
        jnp.ones((8, m.shape[1]), f32), m, (((1,), (1,)), ((), ())),
        preferred_element_type=f32, precision=lax.Precision.HIGHEST,
    )


def proj_kernel(
    sc_ref, pick_ref, att_ref, w_ref, a1, a2, a3, b1, b2, b3, rp_ref, pg_ref, fg_ref,
    own_ref, zp_ref,
):
    zi, ci = sc_ref[0], sc_ref[1]
    heads = [zi * 2, zi * 2 + 1]
    heads += [((zi - s + 4) % 4) * 2 + ci for s in (1, 2, 3)]
    heads += [((zi - s + 4) % 4) * 2 + 1 - ci for s in (1, 2, 3)]
    weights = [w_ref.at[:512], w_ref.at[512:], a1, a2, a3, b1, b2, b3]
    total = None
    for n in range(8):
        lhs = jnp.concatenate([att_ref[heads[n] * 4 + h] for h in range(4)], axis=1)
        part = jnp.dot(lhs, weights[n][...], preferred_element_type=f32)
        total = part if total is None else total + part
    own_ref[...] = total
    own = own_ref[...]
    squares = row_of_sums(lane_sums(own * own))
    for z in range(4):
        for p in range(PICK):
            zp_ref[z, p : p + 1, :] = own_ref[pl.ds(pick_ref[p], 1), :]
        zp_ref[z, 8:16, :] = rp_ref[...]
        zp_ref[z, 16:17, :] = pg_ref[...]
        zp_ref[z, 17:18, :] = fg_ref[...]
        zp_ref[z, 18:24, :] = jnp.zeros((6, COLS), f32)
        zp_ref[z, 18:19, :LOSS_TOKENS] = squares[:1]


def project(scalars, pick, att, w, parts, res_pick, pg, fg):
    whole = lambda *dims: pl.BlockSpec(dims, lambda i, *sc: (0,) * len(dims))
    return pl.pallas_call(
        proj_kernel,
        out_shape=(
            pltpu.MemorySpace.HBM((BLK, COLS), f32),
            pltpu.MemorySpace.HBM((4, 24, COLS), f32),
        ),
        grid_spec=pltpu.PrefetchScalarGridSpec(
            num_scalar_prefetch=2,
            grid=(1,),
            in_specs=[VMEM_SPEC] * 8
            + [whole(PICK, COLS), whole(1, COLS), whole(1, COLS)],
            out_specs=(whole(BLK, COLS), whole(4, 24, COLS)),
        ),
        compiler_params=params(20),
    )(scalars, pick, in_vmem(att), in_vmem(w), *[in_vmem(p) for p in parts], res_pick, pg, fg)


def norm_kernel(zr_ref, ext_ref, out_ref):
    own = [zr_ref[z, :8, :] for z in range(4)]
    total = sum(jnp.sum(o * o, axis=1, keepdims=True) for o in own)
    inv = lax.rsqrt(total / D + epsilon)
    picked = [
        (zr_ref[z, 8:16, :] + own[z] * inv * zr_ref[z, 16:17, :]).astype(bf16).astype(f32)
        for z in range(4)
    ]
    total = sum(jnp.sum(o * o, axis=1, keepdims=True) for o in picked)
    inv = lax.rsqrt(total / D + epsilon)
    for z in range(4):
        normed = (picked[z] * inv * zr_ref[z, 17:18, :]).astype(bf16)
        for n in range(16):
            out_ref[n, :, z * COLS : (z + 1) * COLS] = normed
    for n in range(16):
        out_ref[n, :, D:] = ext_ref[...]


def normalise(zr, ext):
    return pl.pallas_call(
        norm_kernel,
        out_shape=jax.ShapeDtypeStruct((16, PICK, D + EXT), bf16),
        in_specs=[VMEM_SPEC, pl.BlockSpec((PICK, EXT), lambda: (0, 0))],
        compiler_params=pltpu.CompilerParams(vmem_limit_bytes=16 * 1024 * 1024),
    )(in_vmem(zr), ext)


def loss_kernel(sc_ref, g_ref, s_ref, e_ref, own_ref, sib_ref, nbuf, acc, sums):
    j = pl.program_id(0)

    @pl.when(j == 0)
    def _():
        nbuf[:128] = g_ref[...]
        nbuf[128:] = s_ref[...]

    emb = e_ref[...]
    raw = scores(nbuf[:, :D], emb)
    bent = jnp.tanh(raw / logit_cap)
    logits = logit_cap * bent
    big = jnp.exp(logits)
    code = nbuf[:, D:].astype(f32)
    target = code[:, 0:1] * 16384.0 + code[:, 1:2] * 128.0 + code[:, 2:3]
    at = lax.broadcasted_iota(jnp.int32, (LOSS_TOKENS, BLK), 1) + (sc_ref[5] + j * BLK)
    hit = at == target.astype(jnp.int32)
    left = jnp.concatenate(
        [(big * (1.0 - bent * bent)).astype(bf16), jnp.where(hit, 1.0, 0.0).astype(bf16)], axis=0
    )
    both = [lane_sums(big), lane_sums(jnp.where(hit, logits, 0.0))]

    @pl.when(j == 0)
    def _():
        acc[...] = jnp.dot(left, emb, preferred_element_type=f32)
        sums[0], sums[1] = both

    @pl.when(jnp.logical_and(j > 0, j < 3))
    def _():
        acc[...] += jnp.dot(left, emb, preferred_element_type=f32)
        sums[0] += both[0]
        sums[1] += both[1]

    @pl.when(j == 3)
    def _():
        facts = []
        for part in range(2):
            row = row_of_sums(sums[part] + both[part])[:1]
            high = row.astype(bf16).astype(f32)
            facts += [high, row - high]
        first = sc_ref[1] == 0
        half = [jnp.concatenate([r[:, h : h + 128] for r in facts], axis=0) for h in (0, 128)]
        info = jnp.concatenate(
            [jnp.where(first, half[0], half[1]), jnp.where(first, half[1], half[0])], axis=0
        )
        tall = jnp.concatenate([info] * 16, axis=0)
        slots = [jnp.where(first, tall, 0.0), jnp.where(first, 0.0, tall)]
        tall = jnp.concatenate(slots, axis=1).astype(bf16)
        for ref in (own_ref, sib_ref):
            for z in range(4):
                ref[z, :, 2 * COLS :] = tall
        for part in range(2):
            for z in range(4):
                cols = slice(z * COLS, (z + 1) * COLS)
                rows = slice(part * 256, (part + 1) * 256)
                whole = acc[rows, cols] + jnp.dot(
                    left[rows], emb[:, cols], preferred_element_type=f32
                )
                lanes = slice(part * COLS, (part + 1) * COLS)
                own_ref[z, :, lanes] = whole[:128].astype(bf16)
                sib_ref[z, :, lanes] = whole[128:].astype(bf16)


def loss_parts(scalars, g, s, emb):
    whole = lambda *dims: pl.BlockSpec(dims, lambda i, sc: (0,) * len(dims))
    return pl.pallas_call(
        loss_kernel,
        out_shape=(
            jax.ShapeDtypeStruct((4, 128, WIDE), bf16),
            jax.ShapeDtypeStruct((4, 128, WIDE), bf16),
        ),
        grid_spec=pltpu.PrefetchScalarGridSpec(
            num_scalar_prefetch=1,
            grid=(4,),
            in_specs=[
                VMEM_SPEC,
                VMEM_SPEC,
                pl.BlockSpec((BLK, D), lambda i, sc: (i, 0)),
            ],
            out_specs=(whole(4, 128, WIDE), whole(4, 128, WIDE)),
            scratch_shapes=[
                pltpu.VMEM((LOSS_TOKENS, D + EXT), bf16),
                pltpu.VMEM((2 * LOSS_TOKENS, D), f32),
                pltpu.VMEM((2, LOSS_TOKENS, 128), f32),
            ],
        ),
        compiler_params=params(44),
    )(scalars, in_vmem(g), in_vmem(s), emb)


def finish_kernel(sc_ref, back_ref, mask_ref, grad_ref, loss_ref):
    def add(n, sums):
        return sums + back_ref[n].astype(f32)

    sums = lax.fori_loop(1, 64, add, back_ref[0].astype(f32), unroll=7)
    facts = sums[:, 2 * COLS : 2 * COLS + EXT] + sums[:, 2 * COLS + EXT :]
    totals = [facts[n : n + 1] + facts[n + 1 : n + 2] for n in (0, 4)]
    hits = [facts[n : n + 1] + facts[n + 1 : n + 2] for n in (2, 6)]
    masks = [mask_ref[n : n + 1] for n in range(2)]
    loss = [jnp.sum(m * (jnp.log(t) - h)) for m, t, h in zip(masks, totals, hits)]
    loss_ref[0, 0] = (loss[0] + loss[1]) / LOSS_TOKENS
    lane = lax.broadcasted_iota(jnp.int32, (PICK, 128), 1)
    row = lax.broadcasted_iota(jnp.int32, (PICK, 128), 0)
    own = lane == row + sc_ref[6]

    def mine(halves):
        held = jnp.where(sc_ref[1] == 0, halves[0], halves[1])
        return jnp.sum(jnp.where(own, held, 0.0), axis=1, keepdims=True)

    bent = mine(hits) / logit_cap
    slope = 1.0 - bent * bent
    grad_ref[...] = mine(masks) * (sums[:, :COLS] / mine(totals) - slope * sums[:, COLS : 2 * COLS])


def finish(scalars, back, masks):
    return pl.pallas_call(
        finish_kernel,
        out_shape=(
            jax.ShapeDtypeStruct((PICK, COLS), f32),
            jax.ShapeDtypeStruct((1, 1), f32),
        ),
        in_specs=[pl.BlockSpec(memory_space=pltpu.MemorySpace.SMEM), VMEM_SPEC, VMEM_SPEC],
        out_specs=(VMEM_SPEC, pl.BlockSpec(memory_space=pltpu.MemorySpace.SMEM)),
        compiler_params=pltpu.CompilerParams(vmem_limit_bytes=16 * 1024 * 1024),
    )(scalars, in_vmem(back), masks)


def shards(
    query_rows, key_rows, value_rows, residual, out_weight, post_gain, final_gain,
    embedding, targets, loss_mask, pick_pos,
):
    xi, yi, ci, zi = (lax.axis_index(a) for a in ("x", "y", "core", "vocab"))
    base = (((xi * 4 + yi) * 2 + ci) * 4 + zi) * embedding.shape[0]
    scalars = jnp.stack(
        [zi, ci, jnp.where(yi >= 1, 0, 1), jnp.where(yi == 3, 0, 1), jnp.where(yi >= 2, 0, 1), base, (xi * 4 + yi) * PICK]
    ).astype(jnp.int32)

    packed = pack(query_rows, key_rows, value_rows)
    got = exchange(packed, ("x", "core"))
    q = got[:, :BLK].reshape(4, SPAN, HEAD_DIM)
    own = got[:, BLK:].reshape(4 * SPAN, HEAD_DIM)

    swap = lambda a: lax.ppermute(a, "core", SWAP)
    own_pair = [own, swap(own)]
    got_y = []
    for k in (1, 3, 2):
        got_y.append(lax.ppermute(own, "y", ring(k)))
    down, up, far = got_y

    mine = []
    for s in (1, 2, 3):
        part = lax.dynamic_slice(out_weight, (ci * 512, ((zi + s) % 4) * COLS), (512, COLS))
        mine.append(lax.ppermute(part, "vocab", ring(s)))
    theirs = [swap(p) for p in mine]

    acc = attn_call(scalars, q, own_pair)
    acc = attn_call(scalars, q, [down, swap(down)], acc, at=2)
    out = attn_call(scalars, q, [up, swap(up), far, swap(far)], acc, at=3, last=True)
    att = exchange(out.reshape(32, BLK, HEAD_DIM), ("vocab", "x", "core"))
    kept = lax.dynamic_slice(out_weight, (0, zi * COLS), (1024, COLS))

    res_pick = jnp.take(residual, pick_pos, axis=0).astype(f32)
    own_cols, zp = project(
        scalars, pick_pos, att, kept, mine + theirs,
        res_pick, post_gain[None], final_gain[None],
    )
    zr = exchange(zp, "vocab")
    square_sum = jnp.sum(zr[:, 18, :LOSS_TOKENS], axis=0)
    inv_rms = lax.rsqrt(square_sum / D + epsilon)[:, None]
    final_hidden = (residual.astype(f32) + own_cols * inv_rms * post_gain).astype(bf16)

    coded = jnp.stack([targets >> 14, (targets >> 7) & 127, targets & 127, loss_mask], axis=1)
    ext = jnp.pad(coded, ((0, 0), (0, EXT - 4))).astype(bf16)
    normed = normalise(zr, ext)
    g = exchange(normed, ("x", "y")).reshape(128, D + EXT)
    sibling = swap(g)
    own_part, sib_part = loss_parts(scalars, g, sibling, embedding)
    payload = (own_part.astype(f32) + swap(sib_part).astype(f32)).astype(bf16)
    back = exchange(payload.reshape(64, 8, WIDE), ("vocab", "x", "y"))
    held = [g[:, D + 3].astype(f32), sibling[:, D + 3].astype(f32)]
    masks = jnp.where(ci == 0, jnp.stack(held), jnp.stack(held[::-1]))
    grad, loss = finish(scalars, back, masks)
    loss = loss[0, 0]
    return (final_hidden, loss, grad)


def solution(mesh):
    split = Mesh(
        mesh.devices.reshape(4, 4, 2, mesh.shape["vocab"]), ("x", "y", "core", "vocab")
    )

    return jax.shard_map(
        shards,
        mesh=split,
        in_specs=(
            P(CTX, "vocab"),
            P(CTX, "vocab"),
            P(CTX, "vocab"),
            P(CTX, "vocab"),
            P("vocab", None),
            P("vocab"),
            P("vocab"),
            P((*CTX, "vocab"), None),
            P(CTX),
            P(CTX),
            P(CTX),
        ),
        out_specs=(P(CTX, "vocab"), P(), P(CTX, "vocab")),
        check_vma=False,
    )
```

```python
import functools

import jax
import jax.numpy as jnp
from jax import lax
from jax.experimental import pallas as pl
from jax.experimental.pallas import tpu as pltpu
from jax.sharding import Mesh
from jax.sharding import PartitionSpec as P


D = 4608
HEAD_DIM = 128
PICK = 8
SPAN = 512
BLK = 256
COLS = 1152
EXT = 128
WIDE = 2 * COLS + 2 * EXT
LOSS_TOKENS = 256
CTX = ("x", "y", "core")

attn_cap = 50.0
logit_cap = 30.0
query_scalar = 144.0
epsilon = 1e-06

f32 = jnp.float32
bf16 = jnp.bfloat16


def ring(k):
    return [(j, (j + k) % 4) for j in range(4)]


SWAP = [(0, 1), (1, 0)]


def in_vmem(a):
    return pltpu.with_memory_space_constraint(a, pltpu.MemorySpace.VMEM)


def in_hbm(a):
    return pltpu.with_memory_space_constraint(a, pltpu.MemorySpace.HBM)


def params(mib):
    return pltpu.CompilerParams(
        dimension_semantics=("arbitrary",), vmem_limit_bytes=mib * 1024 * 1024
    )


VMEM_SPEC = pl.BlockSpec(memory_space=pltpu.MemorySpace.VMEM)


def pack_kernel(q_ref, k_ref, v_ref, out_ref):
    for h in range(8):
        out_ref[h, :BLK, :] = q_ref[:, h * HEAD_DIM : (h + 1) * HEAD_DIM]
        other = (k_ref, v_ref)[h % 2]
        out_ref[h, BLK:, :] = other[:, h // 2 * HEAD_DIM : (h // 2 + 1) * HEAD_DIM]


def pack(q, k, v):
    whole = lambda *dims: pl.BlockSpec(dims, lambda i: (0,) * len(dims))
    return pl.pallas_call(
        pack_kernel,
        out_shape=pltpu.MemorySpace.HBM((8, SPAN, HEAD_DIM), bf16),
        grid=(1,),
        in_specs=[whole(BLK, 8 * HEAD_DIM), whole(BLK, 4 * HEAD_DIM), whole(BLK, 4 * HEAD_DIM)],
        out_specs=whole(8, SPAN, HEAD_DIM),
    )(q, k, v)


def exchange(pieces, axes):
    return lax.all_to_all(pieces, axes, 0, 0, tiled=True)


def scores(q, k):
    return lax.dot_general(q, k, (((1,), (1,)), ((), ())), preferred_element_type=f32)


def weigh(raw):
    return jnp.exp(attn_cap * jnp.tanh(raw * (query_scalar**-0.5 / attn_cap)))


def lane_sums(p):
    parts = [p[:, i : i + 128] for i in range(0, p.shape[1], 128)]
    return functools.reduce(jnp.add, parts)


def load_kv(core, a_ref, b_ref, buf, sem):
    copies = [
        pltpu.make_async_copy(a_ref, buf.at[core], sem.at[0]),
        pltpu.make_async_copy(b_ref, buf.at[1 - core], sem.at[1]),
    ]
    for copy in copies:
        copy.start()
    return copies


def in_turn(tasks):
    results = []
    raw = tasks[0][0]()
    for n, (_, after) in enumerate(tasks):
        ahead = tasks[n + 1][0]() if n + 1 < len(tasks) else None
        results.append(after(weigh(raw)))
        raw = ahead
    return results


def times_values(p, v):
    return jnp.dot(p.astype(bf16), v, preferred_element_type=f32), lane_sums(p)


def seen(q, buf, first, span, valid=None):
    def before():
        return scores(q, buf[0, pl.ds(first, span), :])

    def after(p):
        if valid is not None:
            p = jnp.where(valid, p, 0.0)
        return times_values(p, buf[1, pl.ds(first, span), :])

    return before, after


def attn_own_kernel(sc_ref, q_ref, a_ref, b_ref, acc_ref, buf, sem):
    i = pl.program_id(0)

    @pl.when(i == 0)
    def _():
        for copy in load_kv(sc_ref[1], a_ref, b_ref, buf, sem):
            copy.wait()

    def body(earlier):
        has_edge = i >= 2
        edge0 = jnp.maximum(i - 2, 0) * SPAN
        diag0 = i * SPAN
        tq = lax.broadcasted_iota(jnp.int32, (BLK, BLK), 0)
        tk = lax.broadcasted_iota(jnp.int32, (BLK, BLK), 1)
        causal = tk <= tq
        beyond = jnp.logical_and(jnp.logical_not(causal), has_edge)
        q = [q_ref[0, pl.ds(r * BLK, BLK), :] for r in range(2)]

        def corner(r):
            def before():
                raw = scores(q[r], buf[0, pl.ds(diag0 + r * BLK, BLK), :])
                if earlier:
                    edge = scores(q[r], buf[0, pl.ds(edge0 + r * BLK, BLK), :])
                    raw = jnp.where(causal, raw, edge)
                return raw

            def after(p):
                pd = jnp.where(causal, p, 0.0)
                top, low = times_values(pd, buf[1, pl.ds(diag0 + r * BLK, BLK), :])
                if earlier:
                    pe = jnp.where(beyond, p, 0.0)
                    more = times_values(pe, buf[1, pl.ds(edge0 + r * BLK, BLK), :])
                    top, low = top + more[0], low + more[1]
                return top, low

            return before, after

        tasks = [corner(0), corner(1), seen(q[1], buf, diag0, BLK)]
        if earlier:
            tasks.append(seen(q[0], buf, edge0 + BLK, BLK, has_edge))
            tasks.append(seen(q_ref[0], buf, (i - 1) * SPAN, SPAN))
        parts = in_turn(tasks)
        for r in range(2):
            for lane in range(2):
                total = parts[r][lane]
                if r == 1:
                    total += parts[2][lane]
                if earlier and r == 0:
                    total += parts[3][lane]
                if earlier:
                    total += parts[4][lane][r * BLK : (r + 1) * BLK]
                acc_ref[0, pl.ds(r * BLK, BLK), lane * HEAD_DIM : (lane + 1) * HEAD_DIM] = total

    pl.when(i == 0)(lambda: body(False))
    pl.when(i > 0)(lambda: body(True))


def attn_more_kernel(chunks, last, at, sc_ref, q_ref, *refs):
    keys, (in_ref, out_ref, buf, sem, *scr) = refs[: 2 * chunks], refs[2 * chunks :]
    i = pl.program_id(0)
    acc_ref = scr[0] if last else out_ref

    @pl.when(i == 0)
    def _():
        copies = []
        for n in range(chunks):
            copies += load_kv(sc_ref[1], keys[2 * n], keys[2 * n + 1], buf.at[n], sem.at[n])
        for copy in copies:
            copy.wait()
        acc_ref[...] = in_ref[...]

    def add(base, tasks):
        for lane, lanes in enumerate((slice(0, HEAD_DIM), slice(HEAD_DIM, 2 * HEAD_DIM))):
            if lane == 0:
                parts = in_turn(tasks)
            total = base[0, :, lanes]
            for part in parts:
                total += part[lane]
            acc_ref[0, :, lanes] = total

    for n in range(chunks):

        @pl.when(jnp.logical_and(i == 0, sc_ref[at + n] == 0))
        def _():
            add(acc_ref, [seen(q_ref[0], buf.at[n], 0, SPAN)])

    @pl.when(i > 0)
    def _():
        tasks = []
        for n in range(chunks):
            newest = i - sc_ref[at + n]
            first = jnp.maximum(newest - 1, 0) * SPAN
            tasks.append(seen(q_ref[0], buf.at[n], first, SPAN))
            tasks.append(seen(q_ref[0], buf.at[n], first + SPAN, SPAN, newest > 0))
        add(in_ref, tasks)

    if last:
        whole = jnp.sum(acc_ref[0, :, HEAD_DIM:], axis=1, keepdims=True)
        done = (acc_ref[0, :, :HEAD_DIM] / whole).astype(bf16)
        for z in range(4):
            for r in range(2):
                out_ref[0, r, z] = done[r * BLK : (r + 1) * BLK]


def attn_call(scalars, q, keys, acc=None, at=0, last=False):
    q_spec = pl.BlockSpec((1, SPAN, HEAD_DIM), lambda i, sc: (i, 0, 0))
    acc_spec = pl.BlockSpec((1, SPAN, 2 * HEAD_DIM), lambda i, sc: (i, 0, 0))
    hbm = pl.BlockSpec(memory_space=pltpu.MemorySpace.HBM)
    chunks = len(keys) // 2
    out_spec, out_shape = acc_spec, jax.ShapeDtypeStruct((4, SPAN, 2 * HEAD_DIM), f32)
    in_specs, args = [q_spec] + [hbm] * len(keys), [q, *keys]
    if acc is None:
        kernel = attn_own_kernel
        scratch = [pltpu.VMEM((2, 4 * SPAN, HEAD_DIM), bf16), pltpu.SemaphoreType.DMA((2,))]
    else:
        in_specs, args = in_specs + [acc_spec], args + [acc]
        kernel = functools.partial(attn_more_kernel, chunks, last, at)
        scratch = [
            pltpu.VMEM((chunks, 2, 4 * SPAN, HEAD_DIM), bf16),
            pltpu.SemaphoreType.DMA((chunks, 2)),
        ]
    if last:
        out_spec = pl.BlockSpec((1, 2, 4, BLK, HEAD_DIM), lambda i, sc: (i, 0, 0, 0, 0))
        out_shape = pltpu.MemorySpace.HBM((4, 2, 4, BLK, HEAD_DIM), bf16)
        scratch = scratch + [pltpu.VMEM((1, SPAN, 2 * HEAD_DIM), f32)]
    return pl.pallas_call(
        kernel,
        out_shape=out_shape,
        grid_spec=pltpu.PrefetchScalarGridSpec(
            num_scalar_prefetch=1,
            grid=(4,),
            in_specs=in_specs,
            out_specs=out_spec,
            scratch_shapes=scratch,
        ),
        cost_estimate=pl.CostEstimate(
            flops=5_000_000_000 * chunks, transcendentals=0, bytes_accessed=4_000_000
        ),
        compiler_params=params(20),
    )(scalars, *args)


def row_of_sums(m):
    return lax.dot_general(
        jnp.ones((8, m.shape[1]), f32), m, (((1,), (1,)), ((), ())),
        preferred_element_type=f32, precision=lax.Precision.HIGHEST,
    )


def proj_kernel(
    sc_ref, pick_ref, att_ref, w_ref, a1, a2, a3, b1, b2, b3, rp_hbm, pg_ref, fg_ref,
    own_ref, zp_ref, rp_ref, sem, wbuf, wsem,
):
    zi, ci = sc_ref[0], sc_ref[1]
    heads = [zi * 2, zi * 2 + 1]
    heads += [((zi - s + 4) % 4) * 2 + ci for s in (1, 2, 3)]
    heads += [((zi - s + 4) % 4) * 2 + 1 - ci for s in (1, 2, 3)]
    rows_in = pltpu.make_async_copy(rp_hbm, rp_ref, sem)
    rows_in.start()
    col = pl.multiple_of(zi * COLS, 128)
    src = [w_ref.at[pl.ds(0, 512), pl.ds(col, COLS)], w_ref.at[pl.ds(512, 512), pl.ds(col, COLS)]]
    src += [a1, a2, a3, b1, b2, b3]
    copies = [pltpu.make_async_copy(src[n], wbuf.at[n], wsem.at[n]) for n in range(8)]
    copies[0].start()
    copies[1].start()
    total = None
    for n in range(8):
        copies[n].wait()
        if n + 2 < 8:
            copies[n + 2].start()
        lhs = jnp.concatenate([att_ref[heads[n] % 2 * 16 + h * 4 + heads[n] // 2] for h in range(4)], axis=1)
        part = jnp.dot(lhs, wbuf[n], preferred_element_type=f32)
        total = part if total is None else total + part
    own_ref[...] = total
    own = own_ref[...]
    squares = row_of_sums(lane_sums(own * own))
    rows_in.wait()
    for z in range(4):
        for p in range(PICK):
            zp_ref[z, p : p + 1, :] = own_ref[pl.ds(pick_ref[p], 1), :]
        zp_ref[z, 8:16, :] = rp_ref[...]
        zp_ref[z, 16:17, :] = pg_ref[...]
        zp_ref[z, 17:18, :] = fg_ref[...]
        zp_ref[z, 18:24, :] = jnp.zeros((6, COLS), f32)
        zp_ref[z, 18:19, :LOSS_TOKENS] = squares[:1]


def project(scalars, pick, att, w, parts, res_pick, pg, fg):
    whole = lambda *dims: pl.BlockSpec(dims, lambda i, *sc: (0,) * len(dims))
    return pl.pallas_call(
        proj_kernel,
        out_shape=(
            pltpu.MemorySpace.HBM((BLK, COLS), f32),
            pltpu.MemorySpace.HBM((4, 24, COLS), f32),
        ),
        grid=(1,),
        in_specs=[pl.BlockSpec(memory_space=pltpu.MemorySpace.SMEM)] * 2
        + [VMEM_SPEC]
        + [pl.BlockSpec(memory_space=pltpu.MemorySpace.HBM)] * 8
        + [whole(1, COLS), whole(1, COLS)],
        out_specs=(whole(BLK, COLS), whole(4, 24, COLS)),
        scratch_shapes=[
            pltpu.VMEM((PICK, COLS), f32),
            pltpu.SemaphoreType.DMA(()),
            pltpu.VMEM((8, 512, COLS), bf16),
            pltpu.SemaphoreType.DMA((8,)),
        ],
        compiler_params=params(20),
    )(
        scalars, pick, in_vmem(att), *[in_hbm(a) for a in (w, *parts, res_pick)], pg, fg,
    )


def norm_kernel(zr_ref, ext_ref, out_ref):
    own = [zr_ref[z, :8, :] for z in range(4)]
    total = sum(jnp.sum(o * o, axis=1, keepdims=True) for o in own)
    inv = lax.rsqrt(total / D + epsilon)
    picked = [
        (zr_ref[z, 8:16, :] + own[z] * inv * zr_ref[z, 16:17, :]).astype(bf16).astype(f32)
        for z in range(4)
    ]
    total = sum(jnp.sum(o * o, axis=1, keepdims=True) for o in picked)
    inv = lax.rsqrt(total / D + epsilon)
    for z in range(4):
        normed = (picked[z] * inv * zr_ref[z, 17:18, :]).astype(bf16)
        for n in range(16):
            out_ref[n, :, z * COLS : (z + 1) * COLS] = normed
    for n in range(16):
        out_ref[n, :, D:] = ext_ref[...]


def normalise(zr, ext):
    return pl.pallas_call(
        norm_kernel,
        out_shape=jax.ShapeDtypeStruct((16, PICK, D + EXT), bf16),
        in_specs=[VMEM_SPEC, pl.BlockSpec((PICK, EXT), lambda: (0, 0))],
        compiler_params=pltpu.CompilerParams(vmem_limit_bytes=16 * 1024 * 1024),
    )(in_vmem(zr), ext)


def loss_kernel(sc_ref, g_ref, s_ref, e_ref, own_ref, sib_ref, nbuf, acc, sums):
    j = pl.program_id(0)

    @pl.when(j == 0)
    def _():
        nbuf[:128] = g_ref[...]
        nbuf[128:] = s_ref[...]

    emb = e_ref[...]
    raw = scores(nbuf[:, :D], emb)
    bent = jnp.tanh(raw / logit_cap)
    logits = logit_cap * bent
    big = jnp.exp(logits)
    code = nbuf[:, D:].astype(f32)
    target = code[:, 0:1] * 16384.0 + code[:, 1:2] * 128.0 + code[:, 2:3]
    at = lax.broadcasted_iota(jnp.int32, (LOSS_TOKENS, BLK), 1) + (sc_ref[5] + j * BLK)
    hit = at == target.astype(jnp.int32)
    left = jnp.concatenate(
        [(big * (1.0 - bent * bent)).astype(bf16), jnp.where(hit, 1.0, 0.0).astype(bf16)], axis=0
    )
    both = [lane_sums(big), lane_sums(jnp.where(hit, logits, 0.0))]

    @pl.when(j == 0)
    def _():
        acc[...] = jnp.dot(left, emb, preferred_element_type=f32)
        sums[0], sums[1] = both

    @pl.when(jnp.logical_and(j > 0, j < 3))
    def _():
        acc[...] += jnp.dot(left, emb, preferred_element_type=f32)
        sums[0] += both[0]
        sums[1] += both[1]

    @pl.when(j == 3)
    def _():
        facts = []
        for part in range(2):
            row = row_of_sums(sums[part] + both[part])[:1]
            high = row.astype(bf16).astype(f32)
            facts += [high, row - high]
        first = sc_ref[1] == 0
        half = [jnp.concatenate([r[:, h : h + 128] for r in facts], axis=0) for h in (0, 128)]
        info = jnp.concatenate(
            [jnp.where(first, half[0], half[1]), jnp.where(first, half[1], half[0])], axis=0
        )
        tall = jnp.concatenate([info] * 16, axis=0)
        slots = [jnp.where(first, tall, 0.0), jnp.where(first, 0.0, tall)]
        tall = jnp.concatenate(slots, axis=1).astype(bf16)
        for ref in (own_ref, sib_ref):
            for z in range(4):
                ref[z, :, 2 * COLS :] = tall
        for part in range(2):
            for z in range(4):
                cols = slice(z * COLS, (z + 1) * COLS)
                rows = slice(part * 256, (part + 1) * 256)
                whole = acc[rows, cols] + jnp.dot(
                    left[rows], emb[:, cols], preferred_element_type=f32
                )
                lanes = slice(part * COLS, (part + 1) * COLS)
                own_ref[z, :, lanes] = whole[:128].astype(bf16)
                sib_ref[z, :, lanes] = whole[128:].astype(bf16)


def loss_parts(scalars, g, s, emb):
    whole = lambda *dims: pl.BlockSpec(dims, lambda i, sc: (0,) * len(dims))
    return pl.pallas_call(
        loss_kernel,
        out_shape=(
            jax.ShapeDtypeStruct((4, 128, WIDE), bf16),
            jax.ShapeDtypeStruct((4, 128, WIDE), bf16),
        ),
        grid_spec=pltpu.PrefetchScalarGridSpec(
            num_scalar_prefetch=1,
            grid=(4,),
            in_specs=[
                VMEM_SPEC,
                VMEM_SPEC,
                pl.BlockSpec((BLK, D), lambda i, sc: (i, 0)),
            ],
            out_specs=(whole(4, 128, WIDE), whole(4, 128, WIDE)),
            scratch_shapes=[
                pltpu.VMEM((LOSS_TOKENS, D + EXT), bf16),
                pltpu.VMEM((2 * LOSS_TOKENS, D), f32),
                pltpu.VMEM((2, LOSS_TOKENS, 128), f32),
            ],
        ),
        compiler_params=params(44),
    )(scalars, in_vmem(g), in_vmem(s), emb)


def finish_kernel(sc_ref, back_ref, mask_ref, grad_ref, loss_ref):
    def add(n, sums):
        return sums + back_ref[n].astype(f32)

    sums = lax.fori_loop(1, 64, add, back_ref[0].astype(f32), unroll=7)
    facts = sums[:, 2 * COLS : 2 * COLS + EXT] + sums[:, 2 * COLS + EXT :]
    totals = [facts[n : n + 1] + facts[n + 1 : n + 2] for n in (0, 4)]
    hits = [facts[n : n + 1] + facts[n + 1 : n + 2] for n in (2, 6)]
    masks = [mask_ref[n : n + 1] for n in range(2)]
    loss = [jnp.sum(m * (jnp.log(t) - h)) for m, t, h in zip(masks, totals, hits)]
    loss_ref[0, 0] = (loss[0] + loss[1]) / LOSS_TOKENS
    lane = lax.broadcasted_iota(jnp.int32, (PICK, 128), 1)
    row = lax.broadcasted_iota(jnp.int32, (PICK, 128), 0)
    own = lane == row + sc_ref[6]

    def mine(halves):
        held = jnp.where(sc_ref[1] == 0, halves[0], halves[1])
        return jnp.sum(jnp.where(own, held, 0.0), axis=1, keepdims=True)

    bent = mine(hits) / logit_cap
    slope = 1.0 - bent * bent
    grad_ref[...] = mine(masks) * (sums[:, :COLS] / mine(totals) - slope * sums[:, COLS : 2 * COLS])


def finish(scalars, back, masks):
    return pl.pallas_call(
        finish_kernel,
        out_shape=(
            jax.ShapeDtypeStruct((PICK, COLS), f32),
            jax.ShapeDtypeStruct((1, 1), f32),
        ),
        in_specs=[pl.BlockSpec(memory_space=pltpu.MemorySpace.SMEM), VMEM_SPEC, VMEM_SPEC],
        out_specs=(VMEM_SPEC, pl.BlockSpec(memory_space=pltpu.MemorySpace.SMEM)),
        compiler_params=pltpu.CompilerParams(vmem_limit_bytes=16 * 1024 * 1024),
    )(scalars, in_vmem(back), masks)


def shards(
    query_rows, key_rows, value_rows, residual, out_weight, post_gain, final_gain,
    embedding, targets, loss_mask, pick_pos,
):
    xi, yi, ci, zi = (lax.axis_index(a) for a in ("x", "y", "core", "vocab"))
    base = (((xi * 4 + yi) * 2 + ci) * 4 + zi) * embedding.shape[0]
    scalars = jnp.stack(
        [zi, ci, jnp.where(yi >= 1, 0, 1), jnp.where(yi == 3, 0, 1), jnp.where(yi >= 2, 0, 1), base, (xi * 4 + yi) * PICK]
    ).astype(jnp.int32)

    packed = pack(query_rows, key_rows, value_rows)
    got = exchange(packed, ("x", "core"))
    q = got[:, :BLK].reshape(4, SPAN, HEAD_DIM)
    own = got[:, BLK:].reshape(4 * SPAN, HEAD_DIM)

    swap = lambda a: lax.ppermute(a, "core", SWAP)
    own_pair = [own, swap(own)]
    got_y = []
    for k in (1, 3, 2):
        got_y.append(lax.ppermute(own, "y", ring(k)))
    down, up, far = got_y

    mine = []
    for s in (1, 2, 3):
        part = lax.dynamic_slice(out_weight, (ci * 512, ((zi + s) % 4) * COLS), (512, COLS))
        mine.append(lax.ppermute(part, "vocab", ring(s)))
    theirs = [swap(p) for p in mine]

    acc = attn_call(scalars, q, own_pair)
    acc = attn_call(scalars, q, [down, swap(down)], acc, at=2)
    out = attn_call(scalars, q, [up, swap(up), far, swap(far)], acc, at=3, last=True)
    att = exchange(out.reshape(32, BLK, HEAD_DIM), ("x", "core", "vocab"))
    res_pick = jnp.take(residual, pick_pos, axis=0).astype(f32)
    own_cols, zp = project(
        scalars, pick_pos, att, out_weight, mine + theirs,
        res_pick, post_gain[None], final_gain[None],
    )
    zr = exchange(zp, "vocab")
    square_sum = jnp.sum(zr[:, 18, :LOSS_TOKENS], axis=0)
    inv_rms = lax.rsqrt(square_sum / D + epsilon)[:, None]
    final_hidden = (residual.astype(f32) + own_cols * inv_rms * post_gain).astype(bf16)

    coded = jnp.stack([targets >> 14, (targets >> 7) & 127, targets & 127, loss_mask], axis=1)
    ext = jnp.pad(coded, ((0, 0), (0, EXT - 4))).astype(bf16)
    normed = normalise(zr, ext)
    g = exchange(normed, ("x", "y")).reshape(128, D + EXT)
    sibling = swap(g)
    own_part, sib_part = loss_parts(scalars, g, sibling, embedding)
    payload = (own_part.astype(f32) + swap(sib_part).astype(f32)).astype(bf16)
    back = exchange(payload.reshape(64, 8, WIDE), ("vocab", "x", "y"))
    held = [g[:, D + 3].astype(f32), sibling[:, D + 3].astype(f32)]
    masks = jnp.where(ci == 0, jnp.stack(held), jnp.stack(held[::-1]))
    grad, loss = finish(scalars, back, masks)
    loss = loss[0, 0]
    return (final_hidden, loss, grad)


def solution(mesh):
    split = Mesh(
        mesh.devices.reshape(4, 4, 2, mesh.shape["vocab"]), ("x", "y", "core", "vocab")
    )

    return jax.shard_map(
        shards,
        mesh=split,
        in_specs=(
            P(CTX, "vocab"),
            P(CTX, "vocab"),
            P(CTX, "vocab"),
            P(CTX, "vocab"),
            P("vocab", None),
            P("vocab"),
            P("vocab"),
            P((*CTX, "vocab"), None),
            P(CTX),
            P(CTX),
            P(CTX),
        ),
        out_specs=(P(CTX, "vocab"), P(), P(CTX, "vocab")),
        check_vma=False,
    )
```

```python
import functools

import jax
import jax.numpy as jnp
from jax import lax
from jax.experimental import pallas as pl
from jax.experimental.pallas import tpu as pltpu
from jax.sharding import Mesh
from jax.sharding import PartitionSpec as P


D = 4608
HEAD_DIM = 128
PICK = 8
SPAN = 512
BLK = 256
COLS = 1152
EXT = 128
WIDE = 2 * COLS + 2 * EXT
LOSS_TOKENS = 256
CTX = ("x", "y", "core")

attn_cap = 50.0
logit_cap = 30.0
query_scalar = 144.0
epsilon = 1e-06

f32 = jnp.float32
bf16 = jnp.bfloat16


def ring(k):
    return [(j, (j + k) % 4) for j in range(4)]


SWAP = [(0, 1), (1, 0)]


def in_vmem(a):
    return pltpu.with_memory_space_constraint(a, pltpu.MemorySpace.VMEM)


def in_hbm(a):
    return pltpu.with_memory_space_constraint(a, pltpu.MemorySpace.HBM)


def params(mib):
    return pltpu.CompilerParams(
        dimension_semantics=("arbitrary",), vmem_limit_bytes=mib * 1024 * 1024
    )


VMEM_SPEC = pl.BlockSpec(memory_space=pltpu.MemorySpace.VMEM)


def by_head(*blocks):
    count = sum(b.shape[1] for b in blocks) // HEAD_DIM

    def kernel(*refs):
        for h in range(count):
            ref, at = refs[h % len(blocks)], h // len(blocks) * HEAD_DIM
            refs[-1][h] = ref[:, at : at + HEAD_DIM]

    whole = lambda *dims: pl.BlockSpec(dims, lambda i: (0,) * len(dims))
    return pl.pallas_call(
        kernel,
        out_shape=pltpu.MemorySpace.HBM((count, BLK, HEAD_DIM), bf16),
        grid=(1,),
        in_specs=[whole(*b.shape) for b in blocks],
        out_specs=whole(count, BLK, HEAD_DIM),
    )(*blocks)


def exchange(pieces, axes):
    return lax.all_to_all(pieces, axes, 0, 0, tiled=True)


def scores(q, k):
    return lax.dot_general(q, k, (((1,), (1,)), ((), ())), preferred_element_type=f32)


def weigh(raw):
    return jnp.exp(attn_cap * jnp.tanh(raw * (query_scalar**-0.5 / attn_cap)))


def lane_sums(p):
    parts = [p[:, i : i + 128] for i in range(0, p.shape[1], 128)]
    return functools.reduce(jnp.add, parts)


def load_kv(core, a_ref, b_ref, buf, sem):
    copies = [
        pltpu.make_async_copy(a_ref, buf.at[core], sem.at[0]),
        pltpu.make_async_copy(b_ref, buf.at[1 - core], sem.at[1]),
    ]
    for copy in copies:
        copy.start()
    return copies


def in_turn(tasks):
    results = []
    raw = tasks[0][0]()
    for n, (_, after) in enumerate(tasks):
        ahead = tasks[n + 1][0]() if n + 1 < len(tasks) else None
        results.append(after(weigh(raw)))
        raw = ahead
    return results


def times_values(p, v):
    return jnp.dot(p.astype(bf16), v, preferred_element_type=f32), lane_sums(p)


def seen(q, buf, first, span, valid=None):
    def before():
        return scores(q, buf[0, pl.ds(first, span), :])

    def after(p):
        if valid is not None:
            p = jnp.where(valid, p, 0.0)
        return times_values(p, buf[1, pl.ds(first, span), :])

    return before, after


def attn_own_kernel(sc_ref, q_ref, a_ref, b_ref, acc_ref, buf, sem):
    i = pl.program_id(0)

    @pl.when(i == 0)
    def _():
        for copy in load_kv(sc_ref[1], a_ref, b_ref, buf, sem):
            copy.wait()

    def body(earlier):
        has_edge = i >= 2
        edge0 = jnp.maximum(i - 2, 0) * SPAN
        diag0 = i * SPAN
        tq = lax.broadcasted_iota(jnp.int32, (BLK, BLK), 0)
        tk = lax.broadcasted_iota(jnp.int32, (BLK, BLK), 1)
        causal = tk <= tq
        beyond = jnp.logical_and(jnp.logical_not(causal), has_edge)
        q = [q_ref[0, pl.ds(r * BLK, BLK), :] for r in range(2)]

        def corner(r):
            def before():
                raw = scores(q[r], buf[0, pl.ds(diag0 + r * BLK, BLK), :])
                if earlier:
                    edge = scores(q[r], buf[0, pl.ds(edge0 + r * BLK, BLK), :])
                    raw = jnp.where(causal, raw, edge)
                return raw

            def after(p):
                pd = jnp.where(causal, p, 0.0)
                top, low = times_values(pd, buf[1, pl.ds(diag0 + r * BLK, BLK), :])
                if earlier:
                    pe = jnp.where(beyond, p, 0.0)
                    more = times_values(pe, buf[1, pl.ds(edge0 + r * BLK, BLK), :])
                    top, low = top + more[0], low + more[1]
                return top, low

            return before, after

        tasks = [corner(0), corner(1), seen(q[1], buf, diag0, BLK)]
        if earlier:
            tasks.append(seen(q[0], buf, edge0 + BLK, BLK, has_edge))
            tasks.append(seen(q_ref[0], buf, (i - 1) * SPAN, SPAN))
        parts = in_turn(tasks)
        for r in range(2):
            for lane in range(2):
                total = parts[r][lane]
                if r == 1:
                    total += parts[2][lane]
                if earlier and r == 0:
                    total += parts[3][lane]
                if earlier:
                    total += parts[4][lane][r * BLK : (r + 1) * BLK]
                acc_ref[0, pl.ds(r * BLK, BLK), lane * HEAD_DIM : (lane + 1) * HEAD_DIM] = total

    pl.when(i == 0)(lambda: body(False))
    pl.when(i > 0)(lambda: body(True))


def attn_more_kernel(chunks, last, at, sc_ref, q_ref, *refs):
    keys, (in_ref, out_ref, buf, sem, *scr) = refs[: 2 * chunks], refs[2 * chunks :]
    i = pl.program_id(0)
    acc_ref = scr[0] if last else out_ref

    @pl.when(i == 0)
    def _():
        copies = []
        for n in range(chunks):
            copies += load_kv(sc_ref[1], keys[2 * n], keys[2 * n + 1], buf.at[n], sem.at[n])
        for copy in copies:
            copy.wait()
        acc_ref[...] = in_ref[...]

    def add(base, tasks):
        for lane, lanes in enumerate((slice(0, HEAD_DIM), slice(HEAD_DIM, 2 * HEAD_DIM))):
            if lane == 0:
                parts = in_turn(tasks)
            total = base[0, :, lanes]
            for part in parts:
                total += part[lane]
            acc_ref[0, :, lanes] = total

    for n in range(chunks):

        @pl.when(jnp.logical_and(i == 0, sc_ref[at + n] == 0))
        def _():
            add(acc_ref, [seen(q_ref[0], buf.at[n], 0, SPAN)])

    @pl.when(i > 0)
    def _():
        tasks = []
        for n in range(chunks):
            newest = i - sc_ref[at + n]
            first = jnp.maximum(newest - 1, 0) * SPAN
            tasks.append(seen(q_ref[0], buf.at[n], first, SPAN))
            tasks.append(seen(q_ref[0], buf.at[n], first + SPAN, SPAN, newest > 0))
        add(in_ref, tasks)

    if last:
        whole = jnp.sum(acc_ref[0, :, HEAD_DIM:], axis=1, keepdims=True)
        done = (acc_ref[0, :, :HEAD_DIM] / whole).astype(bf16)
        for z in range(4):
            for r in range(2):
                out_ref[0, r, z] = done[r * BLK : (r + 1) * BLK]


def attn_call(scalars, q, keys, acc=None, at=0, last=False):
    q_spec = pl.BlockSpec((1, SPAN, HEAD_DIM), lambda i, sc: (i, 0, 0))
    acc_spec = pl.BlockSpec((1, SPAN, 2 * HEAD_DIM), lambda i, sc: (i, 0, 0))
    hbm = pl.BlockSpec(memory_space=pltpu.MemorySpace.HBM)
    chunks = len(keys) // 2
    out_spec, out_shape = acc_spec, jax.ShapeDtypeStruct((4, SPAN, 2 * HEAD_DIM), f32)
    in_specs, args = [q_spec] + [hbm] * len(keys), [q, *keys]
    if acc is None:
        kernel = attn_own_kernel
        scratch = [pltpu.VMEM((2, 4 * SPAN, HEAD_DIM), bf16), pltpu.SemaphoreType.DMA((2,))]
    else:
        in_specs, args = in_specs + [acc_spec], args + [acc]
        kernel = functools.partial(attn_more_kernel, chunks, last, at)
        scratch = [
            pltpu.VMEM((chunks, 2, 4 * SPAN, HEAD_DIM), bf16),
            pltpu.SemaphoreType.DMA((chunks, 2)),
        ]
    if last:
        out_spec = pl.BlockSpec((1, 2, 4, BLK, HEAD_DIM), lambda i, sc: (i, 0, 0, 0, 0))
        out_shape = pltpu.MemorySpace.HBM((4, 2, 4, BLK, HEAD_DIM), bf16)
        scratch = scratch + [pltpu.VMEM((1, SPAN, 2 * HEAD_DIM), f32)]
    return pl.pallas_call(
        kernel,
        out_shape=out_shape,
        grid_spec=pltpu.PrefetchScalarGridSpec(
            num_scalar_prefetch=1,
            grid=(4,),
            in_specs=in_specs,
            out_specs=out_spec,
            scratch_shapes=scratch,
        ),
        cost_estimate=pl.CostEstimate(
            flops=5_000_000_000 * chunks, transcendentals=0, bytes_accessed=4_000_000
        ),
        compiler_params=params(20),
    )(scalars, *args)


def row_of_sums(m):
    return lax.dot_general(
        jnp.ones((8, m.shape[1]), f32), m, (((1,), (1,)), ((), ())),
        preferred_element_type=f32, precision=lax.Precision.HIGHEST,
    )


def proj_kernel(
    sc_ref, pick_ref, att_ref, w_ref, a1, a2, a3, b1, b2, b3, rp_hbm, pg_ref, fg_ref,
    own_ref, zp_ref, rp_ref, sem, wbuf, wsem,
):
    zi, ci = sc_ref[0], sc_ref[1]
    heads = [zi * 2, zi * 2 + 1]
    heads += [((zi - s + 4) % 4) * 2 + ci for s in (1, 2, 3)]
    heads += [((zi - s + 4) % 4) * 2 + 1 - ci for s in (1, 2, 3)]
    rows_in = pltpu.make_async_copy(rp_hbm, rp_ref, sem)
    rows_in.start()
    col = pl.multiple_of(zi * COLS, 128)
    src = [w_ref.at[pl.ds(0, 512), pl.ds(col, COLS)], w_ref.at[pl.ds(512, 512), pl.ds(col, COLS)]]
    src += [a1, a2, a3, b1, b2, b3]
    copies = [pltpu.make_async_copy(src[n], wbuf.at[n], wsem.at[n]) for n in range(8)]
    copies[0].start()
    copies[1].start()
    total = None
    for n in range(8):
        copies[n].wait()
        if n + 2 < 8:
            copies[n + 2].start()
        lhs = jnp.concatenate([att_ref[heads[n] % 2 * 16 + h * 4 + heads[n] // 2] for h in range(4)], axis=1)
        part = jnp.dot(lhs, wbuf[n], preferred_element_type=f32)
        total = part if total is None else total + part
    own_ref[...] = total
    own = own_ref[...]
    squares = row_of_sums(lane_sums(own * own))
    rows_in.wait()
    for z in range(4):
        for p in range(PICK):
            zp_ref[z, p : p + 1, :] = own_ref[pl.ds(pick_ref[p], 1), :]
        zp_ref[z, 8:16, :] = rp_ref[...]
        zp_ref[z, 16:17, :] = pg_ref[...]
        zp_ref[z, 17:18, :] = fg_ref[...]
        zp_ref[z, 18:24, :] = jnp.zeros((6, COLS), f32)
        zp_ref[z, 18:19, :LOSS_TOKENS] = squares[:1]


def project(scalars, pick, att, w, parts, res_pick, pg, fg):
    whole = lambda *dims: pl.BlockSpec(dims, lambda i, *sc: (0,) * len(dims))
    return pl.pallas_call(
        proj_kernel,
        out_shape=(
            pltpu.MemorySpace.HBM((BLK, COLS), f32),
            pltpu.MemorySpace.HBM((4, 24, COLS), f32),
        ),
        grid=(1,),
        in_specs=[pl.BlockSpec(memory_space=pltpu.MemorySpace.SMEM)] * 2
        + [VMEM_SPEC]
        + [pl.BlockSpec(memory_space=pltpu.MemorySpace.HBM)] * 8
        + [whole(1, COLS), whole(1, COLS)],
        out_specs=(whole(BLK, COLS), whole(4, 24, COLS)),
        scratch_shapes=[
            pltpu.VMEM((PICK, COLS), f32),
            pltpu.SemaphoreType.DMA(()),
            pltpu.VMEM((8, 512, COLS), bf16),
            pltpu.SemaphoreType.DMA((8,)),
        ],
        compiler_params=params(20),
    )(
        scalars, pick, in_vmem(att), *[in_hbm(a) for a in (w, *parts, res_pick)], pg, fg,
    )


def norm_kernel(zr_ref, ext_ref, out_ref):
    own = [zr_ref[z, :8, :] for z in range(4)]
    total = sum(jnp.sum(o * o, axis=1, keepdims=True) for o in own)
    inv = lax.rsqrt(total / D + epsilon)
    picked = [
        (zr_ref[z, 8:16, :] + own[z] * inv * zr_ref[z, 16:17, :]).astype(bf16).astype(f32)
        for z in range(4)
    ]
    total = sum(jnp.sum(o * o, axis=1, keepdims=True) for o in picked)
    inv = lax.rsqrt(total / D + epsilon)
    for z in range(4):
        normed = (picked[z] * inv * zr_ref[z, 17:18, :]).astype(bf16)
        for n in range(16):
            out_ref[n, :, z * COLS : (z + 1) * COLS] = normed
    for n in range(16):
        out_ref[n, :, D:] = ext_ref[...]


def normalise(zr, ext):
    return pl.pallas_call(
        norm_kernel,
        out_shape=jax.ShapeDtypeStruct((16, PICK, D + EXT), bf16),
        in_specs=[VMEM_SPEC, pl.BlockSpec((PICK, EXT), lambda: (0, 0))],
        compiler_params=pltpu.CompilerParams(vmem_limit_bytes=16 * 1024 * 1024),
    )(in_vmem(zr), ext)


def loss_kernel(sc_ref, g_ref, s_ref, e_ref, own_ref, sib_ref, nbuf, acc, sums):
    j = pl.program_id(0)

    @pl.when(j == 0)
    def _():
        nbuf[:128] = g_ref[...]
        nbuf[128:] = s_ref[...]

    emb = e_ref[...]
    raw = scores(nbuf[:, :D], emb)
    bent = jnp.tanh(raw / logit_cap)
    logits = logit_cap * bent
    big = jnp.exp(logits)
    code = nbuf[:, D:].astype(f32)
    target = code[:, 0:1] * 16384.0 + code[:, 1:2] * 128.0 + code[:, 2:3]
    at = lax.broadcasted_iota(jnp.int32, (LOSS_TOKENS, BLK), 1) + (sc_ref[5] + j * BLK)
    hit = at == target.astype(jnp.int32)
    left = jnp.concatenate(
        [(big * (1.0 - bent * bent)).astype(bf16), jnp.where(hit, 1.0, 0.0).astype(bf16)], axis=0
    )
    both = [lane_sums(big), lane_sums(jnp.where(hit, logits, 0.0))]

    @pl.when(j == 0)
    def _():
        acc[...] = jnp.dot(left, emb, preferred_element_type=f32)
        sums[0], sums[1] = both

    @pl.when(jnp.logical_and(j > 0, j < 3))
    def _():
        acc[...] += jnp.dot(left, emb, preferred_element_type=f32)
        sums[0] += both[0]
        sums[1] += both[1]

    @pl.when(j == 3)
    def _():
        facts = []
        for part in range(2):
            row = row_of_sums(sums[part] + both[part])[:1]
            high = row.astype(bf16).astype(f32)
            facts += [high, row - high]
        first = sc_ref[1] == 0
        half = [jnp.concatenate([r[:, h : h + 128] for r in facts], axis=0) for h in (0, 128)]
        info = jnp.concatenate(
            [jnp.where(first, half[0], half[1]), jnp.where(first, half[1], half[0])], axis=0
        )
        tall = jnp.concatenate([info] * 16, axis=0)
        slots = [jnp.where(first, tall, 0.0), jnp.where(first, 0.0, tall)]
        tall = jnp.concatenate(slots, axis=1).astype(bf16)
        for ref in (own_ref, sib_ref):
            for z in range(4):
                ref[z, :, 2 * COLS :] = tall
        for part in range(2):
            for z in range(4):
                cols = slice(z * COLS, (z + 1) * COLS)
                rows = slice(part * 256, (part + 1) * 256)
                whole = acc[rows, cols] + jnp.dot(
                    left[rows], emb[:, cols], preferred_element_type=f32
                )
                lanes = slice(part * COLS, (part + 1) * COLS)
                own_ref[z, :, lanes] = whole[:128].astype(bf16)
                sib_ref[z, :, lanes] = whole[128:].astype(bf16)


def loss_parts(scalars, g, s, emb):
    whole = lambda *dims: pl.BlockSpec(dims, lambda i, sc: (0,) * len(dims))
    return pl.pallas_call(
        loss_kernel,
        out_shape=(
            jax.ShapeDtypeStruct((4, 128, WIDE), bf16),
            jax.ShapeDtypeStruct((4, 128, WIDE), bf16),
        ),
        grid_spec=pltpu.PrefetchScalarGridSpec(
            num_scalar_prefetch=1,
            grid=(4,),
            in_specs=[
                VMEM_SPEC,
                VMEM_SPEC,
                pl.BlockSpec((BLK, D), lambda i, sc: (i, 0)),
            ],
            out_specs=(whole(4, 128, WIDE), whole(4, 128, WIDE)),
            scratch_shapes=[
                pltpu.VMEM((LOSS_TOKENS, D + EXT), bf16),
                pltpu.VMEM((2 * LOSS_TOKENS, D), f32),
                pltpu.VMEM((2, LOSS_TOKENS, 128), f32),
            ],
        ),
        compiler_params=params(44),
    )(scalars, in_vmem(g), in_vmem(s), emb)


def finish_kernel(sc_ref, back_ref, mask_ref, grad_ref, loss_ref):
    def add(n, sums):
        return sums + back_ref[n].astype(f32)

    sums = lax.fori_loop(1, 64, add, back_ref[0].astype(f32), unroll=7)
    facts = sums[:, 2 * COLS : 2 * COLS + EXT] + sums[:, 2 * COLS + EXT :]
    totals = [facts[n : n + 1] + facts[n + 1 : n + 2] for n in (0, 4)]
    hits = [facts[n : n + 1] + facts[n + 1 : n + 2] for n in (2, 6)]
    masks = [mask_ref[n : n + 1] for n in range(2)]
    loss = [jnp.sum(m * (jnp.log(t) - h)) for m, t, h in zip(masks, totals, hits)]
    loss_ref[0, 0] = (loss[0] + loss[1]) / LOSS_TOKENS
    lane = lax.broadcasted_iota(jnp.int32, (PICK, 128), 1)
    row = lax.broadcasted_iota(jnp.int32, (PICK, 128), 0)
    own = lane == row + sc_ref[6]

    def mine(halves):
        held = jnp.where(sc_ref[1] == 0, halves[0], halves[1])
        return jnp.sum(jnp.where(own, held, 0.0), axis=1, keepdims=True)

    bent = mine(hits) / logit_cap
    slope = 1.0 - bent * bent
    grad_ref[...] = mine(masks) * (sums[:, :COLS] / mine(totals) - slope * sums[:, COLS : 2 * COLS])


def finish(scalars, back, masks):
    return pl.pallas_call(
        finish_kernel,
        out_shape=(
            jax.ShapeDtypeStruct((PICK, COLS), f32),
            jax.ShapeDtypeStruct((1, 1), f32),
        ),
        in_specs=[pl.BlockSpec(memory_space=pltpu.MemorySpace.SMEM), VMEM_SPEC, VMEM_SPEC],
        out_specs=(VMEM_SPEC, pl.BlockSpec(memory_space=pltpu.MemorySpace.SMEM)),
        compiler_params=pltpu.CompilerParams(vmem_limit_bytes=16 * 1024 * 1024),
    )(scalars, in_vmem(back), masks)


def shards(
    query_rows, key_rows, value_rows, residual, out_weight, post_gain, final_gain,
    embedding, targets, loss_mask, pick_pos,
):
    xi, yi, ci, zi = (lax.axis_index(a) for a in ("x", "y", "core", "vocab"))
    base = (((xi * 4 + yi) * 2 + ci) * 4 + zi) * embedding.shape[0]
    scalars = jnp.stack(
        [zi, ci, jnp.where(yi >= 1, 0, 1), jnp.where(yi == 3, 0, 1), jnp.where(yi >= 2, 0, 1), base, (xi * 4 + yi) * PICK]
    ).astype(jnp.int32)

    packed = by_head(key_rows, value_rows)
    own = exchange(packed, ("x", "core")).reshape(4 * SPAN, HEAD_DIM)
    packed = by_head(query_rows)
    q = exchange(packed, ("x", "core")).reshape(4, SPAN, HEAD_DIM)

    swap = lambda a: lax.ppermute(a, "core", SWAP)
    own_pair = [own, swap(own)]
    got_y = []
    for k in (1, 3, 2):
        got_y.append(lax.ppermute(own, "y", ring(k)))
    down, up, far = got_y

    mine = []
    for s in (1, 2, 3):
        part = lax.dynamic_slice(out_weight, (ci * 512, ((zi + s) % 4) * COLS), (512, COLS))
        mine.append(lax.ppermute(part, "vocab", ring(s)))
    theirs = [swap(p) for p in mine]

    acc = attn_call(scalars, q, own_pair)
    acc = attn_call(scalars, q, [down, swap(down)], acc, at=2)
    out = attn_call(scalars, q, [up, swap(up), far, swap(far)], acc, at=3, last=True)
    att = exchange(out.reshape(32, BLK, HEAD_DIM), ("x", "core", "vocab"))
    res_pick = jnp.take(residual, pick_pos, axis=0).astype(f32)
    own_cols, zp = project(
        scalars, pick_pos, att, out_weight, mine + theirs,
        res_pick, post_gain[None], final_gain[None],
    )
    zr = exchange(zp, "vocab")
    square_sum = jnp.sum(zr[:, 18, :LOSS_TOKENS], axis=0)
    inv_rms = lax.rsqrt(square_sum / D + epsilon)[:, None]
    final_hidden = (residual.astype(f32) + own_cols * inv_rms * post_gain).astype(bf16)

    coded = jnp.stack([targets >> 14, (targets >> 7) & 127, targets & 127, loss_mask], axis=1)
    ext = jnp.pad(coded, ((0, 0), (0, EXT - 4))).astype(bf16)
    normed = normalise(zr, ext)
    g = exchange(normed, ("x", "y")).reshape(128, D + EXT)
    sibling = swap(g)
    own_part, sib_part = loss_parts(scalars, g, sibling, embedding)
    payload = (own_part.astype(f32) + swap(sib_part).astype(f32)).astype(bf16)
    back = exchange(payload.reshape(64, 8, WIDE), ("vocab", "x", "y"))
    held = [g[:, D + 3].astype(f32), sibling[:, D + 3].astype(f32)]
    masks = jnp.where(ci == 0, jnp.stack(held), jnp.stack(held[::-1]))
    grad, loss = finish(scalars, back, masks)
    loss = loss[0, 0]
    return (final_hidden, loss, grad)


def solution(mesh):
    split = Mesh(
        mesh.devices.reshape(4, 4, 2, mesh.shape["vocab"]), ("x", "y", "core", "vocab")
    )

    return jax.shard_map(
        shards,
        mesh=split,
        in_specs=(
            P(CTX, "vocab"),
            P(CTX, "vocab"),
            P(CTX, "vocab"),
            P(CTX, "vocab"),
            P("vocab", None),
            P("vocab"),
            P("vocab"),
            P((*CTX, "vocab"), None),
            P(CTX),
            P(CTX),
            P(CTX),
        ),
        out_specs=(P(CTX, "vocab"), P(), P(CTX, "vocab")),
        check_vma=False,
    )
```

```python
import functools

import jax
import jax.numpy as jnp
from jax import lax
from jax.experimental import pallas as pl
from jax.experimental.pallas import tpu as pltpu
from jax.sharding import Mesh
from jax.sharding import PartitionSpec as P


D = 4608
HEAD_DIM = 128
PICK = 8
SPAN = 512
BLK = 256
COLS = 1152
EXT = 128
WIDE = 2 * COLS + 2 * EXT
LOSS_TOKENS = 256
CTX = ("x", "y", "core")

attn_cap = 50.0
logit_cap = 30.0
query_scalar = 144.0
epsilon = 1e-06

f32 = jnp.float32
bf16 = jnp.bfloat16


def ring(k):
    return [(j, (j + k) % 4) for j in range(4)]


SWAP = [(0, 1), (1, 0)]


def in_vmem(a):
    return pltpu.with_memory_space_constraint(a, pltpu.MemorySpace.VMEM)


def in_hbm(a):
    return pltpu.with_memory_space_constraint(a, pltpu.MemorySpace.HBM)


def params(mib):
    return pltpu.CompilerParams(
        dimension_semantics=("arbitrary",), vmem_limit_bytes=mib * 1024 * 1024
    )


VMEM_SPEC = pl.BlockSpec(memory_space=pltpu.MemorySpace.VMEM)


def by_head(*blocks):
    count = sum(b.shape[1] for b in blocks) // HEAD_DIM

    def kernel(*refs):
        for h in range(count):
            ref, at = refs[h % len(blocks)], h // len(blocks) * HEAD_DIM
            refs[-1][h] = ref[:, at : at + HEAD_DIM]

    whole = lambda *dims: pl.BlockSpec(dims, lambda i: (0,) * len(dims))
    return pl.pallas_call(
        kernel,
        out_shape=pltpu.MemorySpace.HBM((count, BLK, HEAD_DIM), bf16),
        grid=(1,),
        in_specs=[whole(*b.shape) for b in blocks],
        out_specs=whole(count, BLK, HEAD_DIM),
    )(*blocks)


def exchange(pieces, axes):
    return lax.all_to_all(pieces, axes, 0, 0, tiled=True)


def scores(q, k):
    return lax.dot_general(q, k, (((1,), (1,)), ((), ())), preferred_element_type=f32)


def weigh(raw):
    return jnp.exp(attn_cap * jnp.tanh(raw * (query_scalar**-0.5 / attn_cap)))


def lane_sums(p):
    parts = [p[:, i : i + 128] for i in range(0, p.shape[1], 128)]
    return functools.reduce(jnp.add, parts)


def load_kv(core, a_ref, b_ref, buf, sem):
    copies = [
        pltpu.make_async_copy(a_ref, buf.at[core], sem.at[0]),
        pltpu.make_async_copy(b_ref, buf.at[1 - core], sem.at[1]),
    ]
    for copy in copies:
        copy.start()
    return copies


def in_turn(tasks):
    results = []
    raw = tasks[0][0]()
    for n, (_, after) in enumerate(tasks):
        ahead = tasks[n + 1][0]() if n + 1 < len(tasks) else None
        results.append(after(weigh(raw)))
        raw = ahead
    return results


def times_values(p, v):
    return jnp.dot(p.astype(bf16), v, preferred_element_type=f32), lane_sums(p)


def seen(q, buf, first, span, valid=None):
    def before():
        return scores(q, buf[0, pl.ds(first, span), :])

    def after(p):
        if valid is not None:
            p = jnp.where(valid, p, 0.0)
        return times_values(p, buf[1, pl.ds(first, span), :])

    return before, after


def attn_own_kernel(sc_ref, q_ref, a_ref, b_ref, acc_ref, buf, sem):
    i = pl.program_id(0)

    @pl.when(i == 0)
    def _():
        for copy in load_kv(sc_ref[1], a_ref, b_ref, buf, sem):
            copy.wait()

    def body(earlier):
        has_edge = i >= 2
        edge0 = jnp.maximum(i - 2, 0) * SPAN
        diag0 = i * SPAN
        tq = lax.broadcasted_iota(jnp.int32, (BLK, BLK), 0)
        tk = lax.broadcasted_iota(jnp.int32, (BLK, BLK), 1)
        causal = tk <= tq
        beyond = jnp.logical_and(jnp.logical_not(causal), has_edge)
        q = [q_ref[0, pl.ds(r * BLK, BLK), :] for r in range(2)]

        def corner(r):
            def before():
                raw = scores(q[r], buf[0, pl.ds(diag0 + r * BLK, BLK), :])
                if earlier:
                    edge = scores(q[r], buf[0, pl.ds(edge0 + r * BLK, BLK), :])
                    raw = jnp.where(causal, raw, edge)
                return raw

            def after(p):
                pd = jnp.where(causal, p, 0.0)
                top, low = times_values(pd, buf[1, pl.ds(diag0 + r * BLK, BLK), :])
                if earlier:
                    pe = jnp.where(beyond, p, 0.0)
                    more = times_values(pe, buf[1, pl.ds(edge0 + r * BLK, BLK), :])
                    top, low = top + more[0], low + more[1]
                return top, low

            return before, after

        tasks = [corner(0), corner(1), seen(q[1], buf, diag0, BLK)]
        if earlier:
            tasks.append(seen(q[0], buf, edge0 + BLK, BLK, has_edge))
            tasks.append(seen(q_ref[0], buf, (i - 1) * SPAN, SPAN))
        parts = in_turn(tasks)
        for r in range(2):
            for lane in range(2):
                total = parts[r][lane]
                if r == 1:
                    total += parts[2][lane]
                if earlier and r == 0:
                    total += parts[3][lane]
                if earlier:
                    total += parts[4][lane][r * BLK : (r + 1) * BLK]
                acc_ref[0, pl.ds(r * BLK, BLK), lane * HEAD_DIM : (lane + 1) * HEAD_DIM] = total

    pl.when(i == 0)(lambda: body(False))
    pl.when(i > 0)(lambda: body(True))


def attn_more_kernel(chunks, last, at, sc_ref, q_ref, *refs):
    keys, (in_ref, out_ref, buf, sem, *scr) = refs[: 2 * chunks], refs[2 * chunks :]
    i = pl.program_id(0)
    acc_ref = scr[0] if last else out_ref

    @pl.when(i == 0)
    def _():
        copies = []
        for n in range(chunks):
            copies += load_kv(sc_ref[1], keys[2 * n], keys[2 * n + 1], buf.at[n], sem.at[n])
        for copy in copies:
            copy.wait()
        acc_ref[...] = in_ref[...]

    def add(base, tasks):
        for lane, lanes in enumerate((slice(0, HEAD_DIM), slice(HEAD_DIM, 2 * HEAD_DIM))):
            if lane == 0:
                parts = in_turn(tasks)
            total = base[0, :, lanes]
            for part in parts:
                total += part[lane]
            acc_ref[0, :, lanes] = total

    for n in range(chunks):

        @pl.when(jnp.logical_and(i == 0, sc_ref[at + n] == 0))
        def _():
            add(acc_ref, [seen(q_ref[0], buf.at[n], 0, SPAN)])

    @pl.when(i > 0)
    def _():
        tasks = []
        for n in range(chunks):
            newest = i - sc_ref[at + n]
            first = jnp.maximum(newest - 1, 0) * SPAN
            tasks.append(seen(q_ref[0], buf.at[n], first, SPAN))
            tasks.append(seen(q_ref[0], buf.at[n], first + SPAN, SPAN, newest > 0))
        add(in_ref, tasks)

    if last:
        whole = jnp.sum(acc_ref[0, :, HEAD_DIM:], axis=1, keepdims=True)
        done = (acc_ref[0, :, :HEAD_DIM] / whole).astype(bf16)
        for z in range(4):
            for r in range(2):
                out_ref[0, r, z] = done[r * BLK : (r + 1) * BLK]


def attn_call(scalars, q, keys, acc=None, at=0, last=False):
    q_spec = pl.BlockSpec((1, SPAN, HEAD_DIM), lambda i, sc: (i, 0, 0))
    acc_spec = pl.BlockSpec((1, SPAN, 2 * HEAD_DIM), lambda i, sc: (i, 0, 0))
    hbm = pl.BlockSpec(memory_space=pltpu.MemorySpace.HBM)
    chunks = len(keys) // 2
    out_spec, out_shape = acc_spec, jax.ShapeDtypeStruct((4, SPAN, 2 * HEAD_DIM), f32)
    in_specs, args = [q_spec] + [hbm] * len(keys), [q, *keys]
    if acc is None:
        kernel = attn_own_kernel
        scratch = [pltpu.VMEM((2, 4 * SPAN, HEAD_DIM), bf16), pltpu.SemaphoreType.DMA((2,))]
    else:
        in_specs, args = in_specs + [acc_spec], args + [acc]
        kernel = functools.partial(attn_more_kernel, chunks, last, at)
        scratch = [
            pltpu.VMEM((chunks, 2, 4 * SPAN, HEAD_DIM), bf16),
            pltpu.SemaphoreType.DMA((chunks, 2)),
        ]
    if last:
        out_spec = pl.BlockSpec((1, 2, 4, BLK, HEAD_DIM), lambda i, sc: (i, 0, 0, 0, 0))
        out_shape = pltpu.MemorySpace.HBM((4, 2, 4, BLK, HEAD_DIM), bf16)
        scratch = scratch + [pltpu.VMEM((1, SPAN, 2 * HEAD_DIM), f32)]
    return pl.pallas_call(
        kernel,
        out_shape=out_shape,
        grid_spec=pltpu.PrefetchScalarGridSpec(
            num_scalar_prefetch=1,
            grid=(4,),
            in_specs=in_specs,
            out_specs=out_spec,
            scratch_shapes=scratch,
        ),
        cost_estimate=pl.CostEstimate(
            flops=5_000_000_000 * chunks, transcendentals=0, bytes_accessed=4_000_000
        ),
        compiler_params=params(20),
    )(scalars, *args)


def row_of_sums(m):
    return lax.dot_general(
        jnp.ones((8, m.shape[1]), f32), m, (((1,), (1,)), ((), ())),
        preferred_element_type=f32, precision=lax.Precision.HIGHEST,
    )


def proj_kernel(
    sc_ref, pick_ref, att_ref, w_ref, a1, a2, a3, b1, b2, b3, rp_hbm, pg_ref, fg_ref,
    own_ref, zp_ref, rp_ref, sem, wbuf, wsem,
):
    zi, ci = sc_ref[0], sc_ref[1]
    heads = [zi * 2, zi * 2 + 1]
    heads += [((zi - s + 4) % 4) * 2 + ci for s in (1, 2, 3)]
    heads += [((zi - s + 4) % 4) * 2 + 1 - ci for s in (1, 2, 3)]
    rows_in = pltpu.make_async_copy(rp_hbm, rp_ref, sem)
    rows_in.start()
    col = pl.multiple_of(zi * COLS, 128)
    src = [w_ref.at[pl.ds(0, 512), pl.ds(col, COLS)], w_ref.at[pl.ds(512, 512), pl.ds(col, COLS)]]
    src += [a1, a2, a3, b1, b2, b3]
    copies = [
        pltpu.make_async_copy(src[n], wbuf.at[pl.ds(n * 512, 512)], wsem.at[n]) for n in range(8)
    ]
    for copy in copies[:4]:
        copy.start()
    total = None
    for pair in range(4):
        for n in (2 * pair, 2 * pair + 1):
            copies[n].wait()
            if n + 4 < 8:
                copies[n + 4].start()
        lhs = jnp.concatenate(
            [
                att_ref[heads[n] % 2 * 16 + h * 4 + heads[n] // 2]
                for n in (2 * pair, 2 * pair + 1)
                for h in range(4)
            ],
            axis=1,
        )
        rows = slice(pair * 1024, (pair + 1) * 1024)
        part = jnp.dot(lhs, wbuf[rows], preferred_element_type=f32)
        total = part if total is None else total + part
    own_ref[...] = total
    own = own_ref[...]
    squares = row_of_sums(lane_sums(own * own))
    rows_in.wait()
    for z in range(4):
        for p in range(PICK):
            zp_ref[z, p : p + 1, :] = own_ref[pl.ds(pick_ref[p], 1), :]
        zp_ref[z, 8:16, :] = rp_ref[...]
        zp_ref[z, 16:17, :] = pg_ref[...]
        zp_ref[z, 17:18, :] = fg_ref[...]
        zp_ref[z, 18:24, :] = jnp.zeros((6, COLS), f32)
        zp_ref[z, 18:19, :LOSS_TOKENS] = squares[:1]


def project(scalars, pick, att, w, parts, res_pick, pg, fg):
    whole = lambda *dims: pl.BlockSpec(dims, lambda i, *sc: (0,) * len(dims))
    return pl.pallas_call(
        proj_kernel,
        out_shape=(
            pltpu.MemorySpace.HBM((BLK, COLS), f32),
            pltpu.MemorySpace.HBM((4, 24, COLS), f32),
        ),
        grid=(1,),
        in_specs=[pl.BlockSpec(memory_space=pltpu.MemorySpace.SMEM)] * 2
        + [VMEM_SPEC]
        + [pl.BlockSpec(memory_space=pltpu.MemorySpace.HBM)] * 8
        + [whole(1, COLS), whole(1, COLS)],
        out_specs=(whole(BLK, COLS), whole(4, 24, COLS)),
        scratch_shapes=[
            pltpu.VMEM((PICK, COLS), f32),
            pltpu.SemaphoreType.DMA(()),
            pltpu.VMEM((8 * 512, COLS), bf16),
            pltpu.SemaphoreType.DMA((8,)),
        ],
        compiler_params=params(20),
    )(
        scalars, pick, in_vmem(att), *[in_hbm(a) for a in (w, *parts, res_pick)], pg, fg,
    )


def norm_kernel(zr_ref, ext_ref, out_ref):
    own = [zr_ref[z, :8, :] for z in range(4)]
    total = sum(jnp.sum(o * o, axis=1, keepdims=True) for o in own)
    inv = lax.rsqrt(total / D + epsilon)
    picked = [
        (zr_ref[z, 8:16, :] + own[z] * inv * zr_ref[z, 16:17, :]).astype(bf16).astype(f32)
        for z in range(4)
    ]
    total = sum(jnp.sum(o * o, axis=1, keepdims=True) for o in picked)
    inv = lax.rsqrt(total / D + epsilon)
    for z in range(4):
        normed = (picked[z] * inv * zr_ref[z, 17:18, :]).astype(bf16)
        for n in range(16):
            out_ref[n, :, z * COLS : (z + 1) * COLS] = normed
    for n in range(16):
        out_ref[n, :, D:] = ext_ref[...]


def normalise(zr, ext):
    return pl.pallas_call(
        norm_kernel,
        out_shape=jax.ShapeDtypeStruct((16, PICK, D + EXT), bf16),
        in_specs=[VMEM_SPEC, pl.BlockSpec((PICK, EXT), lambda: (0, 0))],
        compiler_params=pltpu.CompilerParams(vmem_limit_bytes=16 * 1024 * 1024),
    )(in_vmem(zr), ext)


def loss_kernel(sc_ref, g_ref, s_ref, e_ref, own_ref, sib_ref, nbuf, acc, sums):
    j = pl.program_id(0)

    @pl.when(j == 0)
    def _():
        nbuf[:128] = g_ref[...]
        nbuf[128:] = s_ref[...]

    emb = e_ref[...]
    raw = scores(nbuf[:, :D], emb)
    bent = jnp.tanh(raw / logit_cap)
    logits = logit_cap * bent
    big = jnp.exp(logits)
    code = nbuf[:, D:].astype(f32)
    target = code[:, 0:1] * 16384.0 + code[:, 1:2] * 128.0 + code[:, 2:3]
    at = lax.broadcasted_iota(jnp.int32, (LOSS_TOKENS, BLK), 1) + (sc_ref[5] + j * BLK)
    hit = at == target.astype(jnp.int32)
    left = jnp.concatenate(
        [(big * (1.0 - bent * bent)).astype(bf16), jnp.where(hit, 1.0, 0.0).astype(bf16)], axis=0
    )
    both = [lane_sums(big), lane_sums(jnp.where(hit, logits, 0.0))]

    @pl.when(j == 0)
    def _():
        acc[...] = jnp.dot(left, emb, preferred_element_type=f32)
        sums[0], sums[1] = both

    @pl.when(jnp.logical_and(j > 0, j < 3))
    def _():
        acc[...] += jnp.dot(left, emb, preferred_element_type=f32)
        sums[0] += both[0]
        sums[1] += both[1]

    @pl.when(j == 3)
    def _():
        facts = []
        for part in range(2):
            row = row_of_sums(sums[part] + both[part])[:1]
            high = row.astype(bf16).astype(f32)
            facts += [high, row - high]
        first = sc_ref[1] == 0
        half = [jnp.concatenate([r[:, h : h + 128] for r in facts], axis=0) for h in (0, 128)]
        info = jnp.concatenate(
            [jnp.where(first, half[0], half[1]), jnp.where(first, half[1], half[0])], axis=0
        )
        tall = jnp.concatenate([info] * 16, axis=0)
        slots = [jnp.where(first, tall, 0.0), jnp.where(first, 0.0, tall)]
        tall = jnp.concatenate(slots, axis=1).astype(bf16)
        for ref in (own_ref, sib_ref):
            for z in range(4):
                ref[z, :, 2 * COLS :] = tall
        for part in range(2):
            for z in range(4):
                cols = slice(z * COLS, (z + 1) * COLS)
                rows = slice(part * 256, (part + 1) * 256)
                whole = acc[rows, cols] + jnp.dot(
                    left[rows], emb[:, cols], preferred_element_type=f32
                )
                lanes = slice(part * COLS, (part + 1) * COLS)
                own_ref[z, :, lanes] = whole[:128].astype(bf16)
                sib_ref[z, :, lanes] = whole[128:].astype(bf16)


def loss_parts(scalars, g, s, emb):
    whole = lambda *dims: pl.BlockSpec(dims, lambda i, sc: (0,) * len(dims))
    return pl.pallas_call(
        loss_kernel,
        out_shape=(
            jax.ShapeDtypeStruct((4, 128, WIDE), bf16),
            jax.ShapeDtypeStruct((4, 128, WIDE), bf16),
        ),
        grid_spec=pltpu.PrefetchScalarGridSpec(
            num_scalar_prefetch=1,
            grid=(4,),
            in_specs=[
                VMEM_SPEC,
                VMEM_SPEC,
                pl.BlockSpec((BLK, D), lambda i, sc: (i, 0)),
            ],
            out_specs=(whole(4, 128, WIDE), whole(4, 128, WIDE)),
            scratch_shapes=[
                pltpu.VMEM((LOSS_TOKENS, D + EXT), bf16),
                pltpu.VMEM((2 * LOSS_TOKENS, D), f32),
                pltpu.VMEM((2, LOSS_TOKENS, 128), f32),
            ],
        ),
        compiler_params=params(44),
    )(scalars, in_vmem(g), in_vmem(s), emb)


def finish_kernel(sc_ref, back_ref, mask_ref, grad_ref, loss_ref):
    def add(n, sums):
        return sums + back_ref[n].astype(f32)

    sums = lax.fori_loop(1, 64, add, back_ref[0].astype(f32), unroll=7)
    facts = sums[:, 2 * COLS : 2 * COLS + EXT] + sums[:, 2 * COLS + EXT :]
    totals = [facts[n : n + 1] + facts[n + 1 : n + 2] for n in (0, 4)]
    hits = [facts[n : n + 1] + facts[n + 1 : n + 2] for n in (2, 6)]
    masks = [mask_ref[n : n + 1] for n in range(2)]
    loss = [jnp.sum(m * (jnp.log(t) - h)) for m, t, h in zip(masks, totals, hits)]
    loss_ref[0, 0] = (loss[0] + loss[1]) / LOSS_TOKENS
    lane = lax.broadcasted_iota(jnp.int32, (PICK, 128), 1)
    row = lax.broadcasted_iota(jnp.int32, (PICK, 128), 0)
    own = lane == row + sc_ref[6]

    def mine(halves):
        held = jnp.where(sc_ref[1] == 0, halves[0], halves[1])
        return jnp.sum(jnp.where(own, held, 0.0), axis=1, keepdims=True)

    bent = mine(hits) / logit_cap
    slope = 1.0 - bent * bent
    grad_ref[...] = mine(masks) * (sums[:, :COLS] / mine(totals) - slope * sums[:, COLS : 2 * COLS])


def finish(scalars, back, masks):
    return pl.pallas_call(
        finish_kernel,
        out_shape=(
            jax.ShapeDtypeStruct((PICK, COLS), f32),
            jax.ShapeDtypeStruct((1, 1), f32),
        ),
        in_specs=[pl.BlockSpec(memory_space=pltpu.MemorySpace.SMEM), VMEM_SPEC, VMEM_SPEC],
        out_specs=(VMEM_SPEC, pl.BlockSpec(memory_space=pltpu.MemorySpace.SMEM)),
        compiler_params=pltpu.CompilerParams(vmem_limit_bytes=16 * 1024 * 1024),
    )(scalars, in_vmem(back), masks)


def shards(
    query_rows, key_rows, value_rows, residual, out_weight, post_gain, final_gain,
    embedding, targets, loss_mask, pick_pos,
):
    xi, yi, ci, zi = (lax.axis_index(a) for a in ("x", "y", "core", "vocab"))
    base = (((xi * 4 + yi) * 2 + ci) * 4 + zi) * embedding.shape[0]
    scalars = jnp.stack(
        [zi, ci, jnp.where(yi >= 1, 0, 1), jnp.where(yi == 3, 0, 1), jnp.where(yi >= 2, 0, 1), base, (xi * 4 + yi) * PICK]
    ).astype(jnp.int32)

    packed = by_head(key_rows, value_rows)
    own = exchange(packed, ("x", "core")).reshape(4 * SPAN, HEAD_DIM)
    packed = by_head(query_rows)
    q = exchange(packed, ("x", "core")).reshape(4, SPAN, HEAD_DIM)

    swap = lambda a: lax.ppermute(a, "core", SWAP)
    own_pair = [own, swap(own)]
    got_y = []
    for k in (1, 3, 2):
        got_y.append(lax.ppermute(own, "y", ring(k)))
    down, up, far = got_y

    mine = []
    for s in (1, 2, 3):
        part = lax.dynamic_slice(out_weight, (ci * 512, ((zi + s) % 4) * COLS), (512, COLS))
        mine.append(lax.ppermute(part, "vocab", ring(s)))
    theirs = [swap(p) for p in mine]

    acc = attn_call(scalars, q, own_pair)
    acc = attn_call(scalars, q, [down, swap(down)], acc, at=2)
    out = attn_call(scalars, q, [up, swap(up), far, swap(far)], acc, at=3, last=True)
    att = exchange(out.reshape(32, BLK, HEAD_DIM), ("x", "core", "vocab"))
    res_pick = jnp.take(residual, pick_pos, axis=0).astype(f32)
    own_cols, zp = project(
        scalars, pick_pos, att, out_weight, mine + theirs,
        res_pick, post_gain[None], final_gain[None],
    )
    zr = exchange(zp, "vocab")
    square_sum = jnp.sum(zr[:, 18, :LOSS_TOKENS], axis=0)
    inv_rms = lax.rsqrt(square_sum / D + epsilon)[:, None]
    final_hidden = (residual.astype(f32) + own_cols * inv_rms * post_gain).astype(bf16)

    coded = jnp.stack([targets >> 14, (targets >> 7) & 127, targets & 127, loss_mask], axis=1)
    ext = jnp.pad(coded, ((0, 0), (0, EXT - 4))).astype(bf16)
    normed = normalise(zr, ext)
    g = exchange(normed, ("x", "y")).reshape(128, D + EXT)
    sibling = swap(g)
    own_part, sib_part = loss_parts(scalars, g, sibling, embedding)
    payload = (own_part.astype(f32) + swap(sib_part).astype(f32)).astype(bf16)
    back = exchange(payload.reshape(64, 8, WIDE), ("vocab", "x", "y"))
    held = [g[:, D + 3].astype(f32), sibling[:, D + 3].astype(f32)]
    masks = jnp.where(ci == 0, jnp.stack(held), jnp.stack(held[::-1]))
    grad, loss = finish(scalars, back, masks)
    loss = loss[0, 0]
    return (final_hidden, loss, grad)


def solution(mesh):
    split = Mesh(
        mesh.devices.reshape(4, 4, 2, mesh.shape["vocab"]), ("x", "y", "core", "vocab")
    )

    return jax.shard_map(
        shards,
        mesh=split,
        in_specs=(
            P(CTX, "vocab"),
            P(CTX, "vocab"),
            P(CTX, "vocab"),
            P(CTX, "vocab"),
            P("vocab", None),
            P("vocab"),
            P("vocab"),
            P((*CTX, "vocab"), None),
            P(CTX),
            P(CTX),
            P(CTX),
        ),
        out_specs=(P(CTX, "vocab"), P(), P(CTX, "vocab")),
        check_vma=False,
    )
```
